512 devices in a mesh: item: 2 (over core), row: 16 (over y, z_lo), col: 16 (over z_hi, x).
Axes of the slice: x: 4, y: 8, z: 8 (z_hi: 4, z_lo: 2; z = z_hi * 2 + z_lo), core: 2. Of those that a mesh axis runs over, the one named last changes fastest.
Arguments:
- latents: bfloat16 [2, 2, 64, 64, 3072], P('item', None, 'row', 'col'), may hold values from -640 to 640
- prompt_rows: bfloat16 [2, 226, 3072], P('item'), may hold values from -640 to 640
- peg_weight: bfloat16 [3, 3, 3072], replicated, may hold values from -1 to 1
- modulation_weight: bfloat16 [512, 6144], P(None, 'col'), may hold values from -0.5 to 0.5
- qkv_weight: bfloat16 [3072, 3, 2048], P(('item', 'row'), None, 'col'), may hold values from -3 to 3
- text_len: int32 [2], P('item'), may hold values from 56 to 226, as said below
- timestep: int32 [2], P('item'), may hold values from 0 to 999
Outputs:
- attended: bfloat16 [2, 2, 64, 64, 2048], P('item', None, 'row', None, 'col')
The draws below stay inside these ranges and needn't reach their ends.
Inputs may be any that keep to these rules, and one draw needn't show every extreme that they name: `text_len`: one item has all 226 text tokens valid; the others have fewer.
All inputs are finite; a program needn't handle non-finite values.
Results may differ from the reference program's by a relative error of at most 0.02.
Values may be sent and summed in bfloat16 or wider, within the bound.
No kernel may reach another device: no remote copies, remote signals or barrier semaphores. Data moves between devices by JAX's collectives and lax.ppermute only.
A program may use at most 64 MiB of HBM per device.

```python
import math
import jax
import jax.numpy as jnp
from jax import lax

D = 3072
HD = 64
TEXT = 226
TEMB = 512
H = 32
FR = 2
ITEMS = 2
GH = 64
GW = 64
NLAT = 8192
N_ROW = 16


def scaled_rows(key, shape):
    first, second, third = jax.random.split(key, 3)
    base = jnp.clip(jax.random.normal(first, shape, jnp.float32), -4.0, 4.0)
    row_scale = jnp.exp(jax.random.uniform(second, shape[:-1] + (1,), jnp.float32, 0.0, math.log(10.0)))
    col_scale = jnp.exp(jax.random.uniform(third, shape[-1:], jnp.float32, 0.0, math.log(10.0)))
    return base * row_scale * col_scale


def draw_latents(key, part):
    return scaled_rows(jax.random.fold_in(key, 11), (ITEMS, FR, GH, GW, D)).astype(jnp.bfloat16)


def draw_prompt_rows(key, part):
    return scaled_rows(jax.random.fold_in(key, 23), (ITEMS, TEXT, D)).astype(jnp.bfloat16)


def draw_qkv_weight(key, part):
    first, second, third = jax.random.split(jax.random.fold_in(key, 37), 3)
    shape = (D, H * HD)
    norm_scale = 1.0 / math.sqrt(D)
    query_part = jnp.clip(jax.random.normal(first, shape, jnp.float32), -5.0, 5.0) * (1.7 * norm_scale)
    key_part = jnp.clip(jax.random.normal(second, shape, jnp.float32), -5.0, 5.0) * (1.7 * norm_scale)
    value_part = jnp.clip(jax.random.normal(third, shape, jnp.float32), -5.0, 5.0) * norm_scale
    return jnp.stack([query_part, key_part, value_part], axis=1).astype(jnp.bfloat16)


def draw_text_len(key, part):
    first, second = jax.random.split(jax.random.fold_in(key, 53))
    others = jax.random.randint(first, (ITEMS - 1,), TEXT // 4, TEXT, dtype=jnp.int32)
    lengths = jnp.concatenate([jnp.full((1,), TEXT, dtype=jnp.int32), others])
    return jax.random.permutation(second, lengths)


def shard_levels(rng, extent, shards, smallest, high):
    gain, own = 1.0, jax.random.fold_in(rng, 6)
    for axis_at, blocks in shards:
        heights = jnp.exp(jax.random.uniform(jax.random.fold_in(own, axis_at), (blocks,), jnp.float32, smallest / len(shards), high / len(shards)))
        gain = gain * jnp.repeat(heights, extent[axis_at] // blocks).reshape([-1 if axis == axis_at else 1 for axis in range(len(extent))])
    return gain


def gaussian(stream_key, extent, width, most, cuts=(), kind=jnp.bfloat16):
    entries = jax.random.normal(stream_key, extent, jnp.float32) * width
    if len(cuts) > 0:
        entries = shard_levels(stream_key, extent, cuts, -0.22, 0.18) * entries
    return jnp.clip(entries, min=-most, max=most).astype(kind)


def setup_inputs(seed: int = 0) -> dict:
    seeds = jax.random.split(jax.random.key(seed), 8)
    latents = draw_latents(jax.random.fold_in(seeds[7], 71), 0)
    prompt_rows = draw_prompt_rows(jax.random.fold_in(seeds[7], 71), 0)
    peg_weight = gaussian(seeds[2], (3, 3, D), 0.2, 1.0)
    modulation_weight = gaussian(seeds[3], (TEMB, 2 * D), (TEMB // 4) ** -0.5, 0.5, ((1, 16),))
    qkv_weight = draw_qkv_weight(jax.random.fold_in(seeds[7], 71), 0)
    text_len = draw_text_len(jax.random.fold_in(seeds[7], 71), 0)
    timestep = jax.random.randint(seeds[6], (ITEMS,), 0, 1000).astype(jnp.int32)
    return dict(latents=latents, prompt_rows=prompt_rows, peg_weight=peg_weight, modulation_weight=modulation_weight, qkv_weight=qkv_weight, text_len=text_len, timestep=timestep)


def time_angles(step, count):
    half = count // 2
    freqs = jnp.exp(-math.log(10000.0) * jnp.arange(half, dtype=jnp.float32) / half)
    angle = step.astype(jnp.float32) * freqs
    return jnp.concatenate([jnp.cos(angle), jnp.sin(angle)])

def modulate(rows, shift, scale):
    values = rows.astype(jnp.float32)
    center = lax.optimization_barrier(jnp.mean(values, axis=-1, keepdims=True))
    centered = values - center
    spread = lax.optimization_barrier(jnp.mean(centered * centered, axis=-1, keepdims=True))
    return (centered * lax.rsqrt(spread + 1e-06) * (1.0 + scale) + shift).astype(jnp.bfloat16)

def reference(latents, prompt_rows, peg_weight, modulation_weight, qkv_weight, text_len, timestep):
    flat_weight = qkv_weight.reshape(D, 3 * H * HD)
    results = []
    for item in range(ITEMS):
        frames = latents[item].astype(jnp.float32)
        padded = jnp.pad(frames, ((0, 0), (1, 1), (1, 1), (0, 0)))
        summed = frames
        for row_tap in range(3):
            for col_tap in range(3):
                summed = summed + padded[:, row_tap:row_tap + GH, col_tap:col_tap + GW, :] * peg_weight[row_tap, col_tap].astype(jnp.float32)
        convolved = summed.astype(jnp.bfloat16)
        activation = jax.nn.silu(time_angles(timestep[item], TEMB)).astype(jnp.bfloat16)
        modulation = jnp.dot(activation[None, :], modulation_weight, preferred_element_type=jnp.float32)[0]
        shift = modulation[:D]
        scale = modulation[D:]
        normed = modulate(convolved.reshape(NLAT, D), shift, scale)
        text_normed = modulate(prompt_rows[item], shift, scale)
        latent_qkv = jnp.dot(normed, flat_weight, preferred_element_type=jnp.float32).astype(jnp.bfloat16).reshape(NLAT, 3, H, HD)
        text_qkv = jnp.dot(text_normed, flat_weight, preferred_element_type=jnp.float32).astype(jnp.bfloat16).reshape(TEXT, 3, H, HD)
        key_all = jnp.concatenate([text_qkv[:, 1], latent_qkv[:, 1]], axis=0)
        value_all = jnp.concatenate([text_qkv[:, 2], latent_qkv[:, 2]], axis=0)
        positions = jnp.arange(TEXT + NLAT, dtype=jnp.int32)
        valid = (positions >= TEXT) | (positions < text_len[item])
        query_heads = jnp.transpose(latent_qkv[:, 0], (1, 0, 2))
        key_heads = jnp.transpose(key_all, (1, 0, 2))
        value_heads = jnp.transpose(value_all, (1, 0, 2))

        def one_head(triple):
            queries, key_rows, value_rows = triple
            key_float = key_rows.astype(jnp.float32)

            def one_group(block):
                scores = jnp.dot(block.astype(jnp.float32), key_float.T, precision=lax.Precision.HIGHEST) * 0.125
                scores = jnp.where(valid[None, :], scores, -jnp.inf)
                weights = jnp.exp(scores - lax.optimization_barrier(jnp.max(scores, axis=1, keepdims=True)))
                weighted = jnp.dot(weights.astype(jnp.bfloat16), value_rows, preferred_element_type=jnp.float32)
                return weighted / lax.optimization_barrier(jnp.sum(weights, axis=1, keepdims=True))
            grouped = lax.map(one_group, queries.reshape(N_ROW, NLAT // N_ROW, HD))
            return grouped.reshape(NLAT, HD)
        head_out = lax.map(one_head, (query_heads, key_heads, value_heads))
        attended = jnp.transpose(head_out, (1, 0, 2)).reshape(FR, GH, GW, H * HD).astype(jnp.bfloat16)
        results.append(attended)
    return jnp.stack(results, axis=0)
```

```python
import functools
import math

import jax
import jax.numpy as jnp
from jax import lax
from jax.experimental import pallas as pl
from jax.experimental.pallas import tpu as pltpu
from jax.sharding import Mesh, PartitionSpec as P

HD = 64
LOG2E = 1.4426950408889634
SCALE2 = 0.125 * LOG2E
BF = jnp.bfloat16
F32 = jnp.float32
TEXT_PART = 64


def vmem(*shape):
    return pl.BlockSpec(memory_space=pltpu.VMEM)


def params(mib):
    return pltpu.CompilerParams(vmem_limit_bytes=mib << 20)


def with_halo(block, sides, width):
    for axis, dim in sides:
        count = lax.axis_size(axis)
        forward = [(i, i + 1) for i in range(count - 1)]
        backward = [(target, source) for source, target in forward]
        low = lax.ppermute(
            lax.slice_in_dim(block, block.shape[dim] - width, None, axis=dim), axis, forward
        )
        high = lax.ppermute(lax.slice_in_dim(block, 0, width, axis=dim), axis, backward)
        block = jnp.concatenate([low, block, high], axis=dim)
    return block


def time_angles(step, count):
    half = count // 2
    freqs = jnp.exp(-math.log(10000.0) * jnp.arange(half, dtype=F32) / half)
    angle = step.astype(F32) * freqs
    return jnp.concatenate([jnp.cos(angle), jnp.sin(angle)])


def project_kernel(x_ref, mod_ref, w_ref, *outs):
    values = x_ref[...].astype(F32)
    width = values.shape[1]
    center = jnp.sum(values, axis=1, keepdims=True) * (1.0 / width)
    centered = values - center
    spread = jnp.sum(centered * centered, axis=1, keepdims=True) * (1.0 / width)
    normed = centered * lax.rsqrt(spread + 1e-06) * (1.0 + mod_ref[1:2, :]) + mod_ref[0:1, :]
    rows = jnp.dot(normed.astype(BF), w_ref[...], preferred_element_type=F32).astype(BF)
    at = 0
    for out in outs:
        size = out.shape[1]
        first = rows.shape[1] - sum(o.shape[1] for o in outs) + at
        out[...] = rows[:, first : first + size]
        at += size


def project(x, mod, weight, sizes):
    rows = x.shape[0]
    return pl.pallas_call(
        project_kernel,
        out_shape=[jax.ShapeDtypeStruct((rows, size), BF) for size in sizes],
        in_specs=[vmem()] * 3,
        out_specs=[vmem()] * len(sizes),
        compiler_params=params(24),
        cost_estimate=pl.CostEstimate(
            flops=2 * rows * x.shape[1] * weight.shape[1],
            bytes_accessed=2 * (x.size + weight.size),
            transcendentals=rows,
        ),
        name="project",
    )(x, mod, weight)


def attend_kernel(info, q0, q1, q2, q3, kv, text_kv, o0, o1, o2, o3, values, text_values, *, tile):
    count = kv.shape[0]
    values[:, :128] = kv[:, 128:]
    values[:, 128:] = jnp.ones((count, 128), BF)
    text_values[:, :128] = text_kv[:, 128:]
    text_values[:, 128:] = jnp.ones((TEXT_PART, 128), BF)
    contract = (((1,), (1,)), ((), ()))
    lane = lax.broadcasted_iota(jnp.int32, (tile, 128), 1)
    position = info[0] + lax.broadcasted_iota(jnp.int32, (tile, TEXT_PART), 1)
    valid = (position >= info[1]) & (position < info[2])
    for q_ref, o_ref in ((q0, o0), (q1, o1), (q2, o2), (q3, o3)):

        @pl.loop(0, q_ref.shape[0] // tile)
        def _(step):
            rows = pl.ds(pl.multiple_of(step * tile, tile), tile)
            q = q_ref[rows, :].astype(F32)
            outs, sums = [], []
            for head in range(2):
                own = jnp.where(lane // HD == head, q, 0.0).astype(BF)
                s = lax.dot_general(own, kv[:, :128], contract, preferred_element_type=F32)
                t = lax.dot_general(own, text_kv[:, :128], contract, preferred_element_type=F32)
                t = jnp.where(valid, t, -1e30)
                top = jnp.maximum(
                    jnp.max(s, axis=1, keepdims=True), jnp.max(t, axis=1, keepdims=True)
                )
                top = top * SCALE2
                p = jnp.exp2(s * SCALE2 - top).astype(BF)
                pt = jnp.where(valid, jnp.exp2(t * SCALE2 - top), 0.0).astype(BF)
                acc = jnp.dot(p, values[...], preferred_element_type=F32)
                acc = acc + jnp.dot(pt, text_values[...], preferred_element_type=F32)
                total = acc[:, 128:]
                outs.append(acc[:, :128] / total)
                sums.append(top + jnp.log(total) * LOG2E)
            o_ref[rows, :128] = jnp.where(lane < HD, outs[0], outs[1]).astype(BF)
            stats = jnp.zeros((tile, 128), F32)
            for head in range(2):
                rest = sums[head]
                for part in range(3):
                    piece = rest.astype(BF).astype(F32)
                    stats = jnp.where(lane == 3 * head + part, piece, stats)
                    rest = rest - piece
            o_ref[rows, 128:] = stats.astype(BF)


def attend(info, qs, kv, text_kv):
    count = qs[0].shape[0]
    keys = kv.shape[0]
    return pl.pallas_call(
        functools.partial(attend_kernel, tile=128),
        out_shape=[jax.ShapeDtypeStruct((count, 256), BF)] * 4,
        in_specs=[pl.BlockSpec(memory_space=pltpu.SMEM)] + [vmem()] * 6,
        out_specs=[vmem()] * 4,
        scratch_shapes=[pltpu.VMEM((keys, 256), BF), pltpu.VMEM((TEXT_PART, 256), BF)],
        compiler_params=params(40),
        cost_estimate=pl.CostEstimate(
            flops=4 * 4 * count * (keys + TEXT_PART) * 256,
            bytes_accessed=2 * 256 * (6 * count + keys),
            transcendentals=8 * count * (keys + TEXT_PART),
        ),
        name="attend",
    )(info, *qs, kv, text_kv)


def combine_kernel(slots, p0, p1, p2, p3, out):
    parts = [p[...].astype(F32) for p in (p0, p1, p2, p3)]
    lane = lax.broadcasted_iota(jnp.int32, (parts[0].shape[0], 128), 1)
    lses = []
    for part in parts:
        heads = [
            part[:, 128 + 3 * h : 129 + 3 * h]
            + part[:, 129 + 3 * h : 130 + 3 * h]
            + part[:, 130 + 3 * h : 131 + 3 * h]
            for h in range(2)
        ]
        lses.append(jnp.where(lane < HD, heads[0], heads[1]))
    top = functools.reduce(jnp.maximum, lses)
    shares = [jnp.exp2(lse - top) for lse in lses]
    total = sum(shares)
    weighted = sum(share * part[:, :128] for share, part in zip(shares, parts))
    out[...] = (weighted / total).astype(BF)


def combine(slots, parts):
    count = parts[0].shape[0]
    block = count // 4
    return pl.pallas_call(
        combine_kernel,
        out_shape=jax.ShapeDtypeStruct((count, 128), BF),
        grid_spec=pltpu.PrefetchScalarGridSpec(
            num_scalar_prefetch=1,
            grid=(4,),
            in_specs=[pl.BlockSpec((block, 256), lambda i, slots: (slots[i], 0))] * 4,
            out_specs=pl.BlockSpec((block, 128), lambda i, slots: (i, 0)),
        ),
        compiler_params=params(8),
        name="combine",
    )(slots, *parts)


def on_device(latents, prompt_rows, peg_weight, modulation_weight, qkv_weight, text_len, timestep):
    frames, tile_h, tile_w, width = latents.shape[1:]
    rows_axes = ("u", "v", "zl")
    head_width = qkv_weight.shape[2]
    weight = lax.all_gather(
        qkv_weight.reshape(qkv_weight.shape[0], 3 * head_width),
        ("item",) + rows_axes,
        axis=0,
        tiled=True,
    )
    padded = with_halo(latents, ((rows_axes, 2), (("zh", "x"), 3)), 1)
    summed = latents.astype(F32)
    for row_tap in range(3):
        for col_tap in range(3):
            summed = summed + padded[
                :, :, row_tap : row_tap + tile_h, col_tap : col_tap + tile_w, :
            ].astype(F32) * peg_weight[row_tap, col_tap].astype(F32)
    peg = summed.astype(BF).reshape(frames * tile_h * tile_w, width)
    tokens = lax.all_gather(peg, "zh", axis=0, tiled=True)
    blocks = [tokens] + [
        lax.ppermute(tokens, "x", [(i, (i + k) % 4) for i in range(4)]) for k in (1, 3, 2)
    ]
    activation = jax.nn.silu(time_angles(timestep[0], modulation_weight.shape[0])).astype(BF)
    own_columns = jnp.dot(activation[None, :], modulation_weight, preferred_element_type=F32)
    modulation = lax.all_gather(own_columns, "x", axis=1, tiled=True)
    modulation = lax.all_gather(modulation, "zh", axis=1, tiled=True)
    modulation = modulation.reshape(2, width)

    member = lax.axis_index("v") * 2 + lax.axis_index("zl")
    lower = member * TEXT_PART
    start = jnp.minimum(lower, prompt_rows.shape[1] - TEXT_PART)
    text_rows = lax.dynamic_slice_in_dim(prompt_rows[0], start, TEXT_PART, axis=0)
    (text_kv,) = project(text_rows, modulation, weight, (2 * head_width,))
    projected = [project(block, modulation, weight, (head_width, 2 * head_width)) for block in blocks]
    queries = jnp.concatenate([q for q, _ in projected], axis=0)
    kv = jnp.concatenate([pair for _, pair in projected], axis=0)

    swaps = (
        ("zl", [(0, 1), (1, 0)]),
        ("v", [(0, 1), (1, 0)]),
        (("v", "zl"), [(0, 3), (3, 0), (1, 2), (2, 1)]),
    )
    qs = [queries] + [lax.ppermute(queries, axis, swap) for axis, swap in swaps]
    all_kv = lax.all_gather(kv, "u", axis=0, tiled=True)
    info = jnp.stack([start, lower, text_len[0]])
    parts = attend(info, qs, all_kv, text_kv)
    parts = [parts[0]] + [
        lax.ppermute(part, axis, swap) for part, (axis, swap) in zip(parts[1:], swaps)
    ]
    x_at = lax.axis_index("x")
    slots = jnp.array([0, 2, 3, 1], jnp.int32)[(jnp.arange(4, dtype=jnp.int32) - x_at) % 4]
    attended = combine(slots, parts)
    attended = attended.reshape(4, 4, frames, tile_h, tile_w, head_width)
    attended = attended.transpose(2, 3, 1, 0, 4, 5)
    return attended.reshape(1, frames, tile_h, 16 * tile_w, head_width)


def solution(mesh):
    fine = Mesh(mesh.devices.reshape(2, 4, 2, 2, 4, 4), ("item", "u", "v", "zl", "zh", "x"))
    row = ("u", "v", "zl")
    col = ("zh", "x")
    in_specs = (
        P("item", None, row, col, None),
        P("item", None, None),
        P(),
        P(None, col),
        P(("item",) + row, None, col),
        P("item"),
        P("item"),
    )
    out_specs = P("item", None, row, None, col)
    return jax.shard_map(
        on_device, mesh=fine, in_specs=in_specs, out_specs=out_specs, check_vma=False
    )
```

```python
import functools
import math

import jax
import jax.numpy as jnp
from jax import lax
from jax.experimental import pallas as pl
from jax.experimental.pallas import tpu as pltpu
from jax.sharding import Mesh, PartitionSpec as P

HD = 64
LOG2E = 1.4426950408889634
SCALE2 = 0.125 * LOG2E
BF = jnp.bfloat16
F32 = jnp.float32
TEXT_PART = 64
STAT_ROWS = 16


def vmem(*shape):
    return pl.BlockSpec(memory_space=pltpu.VMEM)


def params(mib):
    return pltpu.CompilerParams(vmem_limit_bytes=mib << 20)


def with_halo(block, sides, width):
    for axis, dim in sides:
        count = lax.axis_size(axis)
        forward = [(i, i + 1) for i in range(count - 1)]
        backward = [(target, source) for source, target in forward]
        low = lax.ppermute(
            lax.slice_in_dim(block, block.shape[dim] - width, None, axis=dim), axis, forward
        )
        high = lax.ppermute(lax.slice_in_dim(block, 0, width, axis=dim), axis, backward)
        block = jnp.concatenate([low, block, high], axis=dim)
    return block


def time_angles(step, count):
    half = count // 2
    freqs = jnp.exp(-math.log(10000.0) * jnp.arange(half, dtype=F32) / half)
    angle = step.astype(F32) * freqs
    return jnp.concatenate([jnp.cos(angle), jnp.sin(angle)])


def project_kernel(x_ref, mod_ref, w_ref, *outs):
    values = x_ref[...].astype(F32)
    width = values.shape[1]
    center = jnp.sum(values, axis=1, keepdims=True) * (1.0 / width)
    centered = values - center
    spread = jnp.sum(centered * centered, axis=1, keepdims=True) * (1.0 / width)
    normed = centered * lax.rsqrt(spread + 1e-06) * (1.0 + mod_ref[1:2, :]) + mod_ref[0:1, :]
    rows = jnp.dot(normed.astype(BF), w_ref[...], preferred_element_type=F32).astype(BF)
    at = 0
    for out in outs:
        size = out.shape[1]
        first = rows.shape[1] - sum(o.shape[1] for o in outs) + at
        out[...] = rows[:, first : first + size]
        at += size


def project(x, mod, weight, sizes):
    rows = x.shape[0]
    return pl.pallas_call(
        project_kernel,
        out_shape=[jax.ShapeDtypeStruct((rows, size), BF) for size in sizes],
        in_specs=[vmem()] * 3,
        out_specs=[vmem()] * len(sizes),
        compiler_params=params(16),
        cost_estimate=pl.CostEstimate(
            flops=2 * rows * x.shape[1] * weight.shape[1],
            bytes_accessed=2 * (x.size + weight.size),
            transcendentals=rows,
        ),
        name="project",
    )(x, mod, weight)


def softmax_tile(q, keys, values, text, valid):
    contract = (((1,), (1,)), ((), ()))
    lane = lax.broadcasted_iota(jnp.int32, (q.shape[0], 128), 1)
    outs, sums = [], []
    for head in range(2):
        own = jnp.where(lane // HD == head, q, 0.0).astype(BF)
        s = lax.dot_general(own, keys, contract, preferred_element_type=F32)
        top = jnp.max(s, axis=1, keepdims=True)
        if text is not None:
            t = lax.dot_general(own, text[0], contract, preferred_element_type=F32)
            t = jnp.where(valid, t, -1e30)
            top = jnp.maximum(top, jnp.max(t, axis=1, keepdims=True))
        top = top * SCALE2
        p = jnp.exp2(s * SCALE2 - top).astype(BF)
        acc = jnp.dot(p, values, preferred_element_type=F32)
        if text is not None:
            pt = jnp.where(valid, jnp.exp2(t * SCALE2 - top), 0.0).astype(BF)
            acc = acc + jnp.dot(pt, text[1], preferred_element_type=F32)
        total = acc[:, 128:]
        outs.append(acc[:, :128] / total)
        sums.append(top + jnp.log(total) * LOG2E)
    return jnp.where(lane < HD, outs[0], outs[1]), jnp.where(lane < HD, sums[0], sums[1])


def first_kernel(info, q0, q1, q2, q3, kv, text_kv, o_ref, l_ref, values, text_values, *, tile):
    count = q0.shape[0]
    values[:, :128] = kv[:, 128:]
    values[:, 128:] = jnp.ones((kv.shape[0], 128), BF)
    text_values[:, :128] = text_kv[:, 128:]
    text_values[:, 128:] = jnp.ones((TEXT_PART, 128), BF)
    position = info[0] + lax.broadcasted_iota(jnp.int32, (tile, TEXT_PART), 1)
    valid = (position >= info[1]) & (position < info[2])
    for member, q_ref in enumerate((q0, q1, q2, q3)):

        @pl.loop(0, count // tile)
        def _(step):
            rows = pl.ds(pl.multiple_of(step * tile, tile), tile)
            out, lse = softmax_tile(
                q_ref[rows, :].astype(F32),
                kv[:, :128],
                values[...],
                (text_kv[:, :128], text_values[...]),
                valid,
            )
            o_ref[member, rows, :] = out
            l_ref[member, rows, :] = lse


def attend_first(info, qs, kv, text_kv):
    count = qs[0].shape[0]
    keys = kv.shape[0]
    return pl.pallas_call(
        functools.partial(first_kernel, tile=128),
        out_shape=[jax.ShapeDtypeStruct((4, count, 128), F32)] * 2,
        in_specs=[pl.BlockSpec(memory_space=pltpu.SMEM)] + [vmem()] * 6,
        out_specs=[vmem()] * 2,
        scratch_shapes=[pltpu.VMEM((keys, 256), BF), pltpu.VMEM((TEXT_PART, 256), BF)],
        compiler_params=params(16),
        cost_estimate=pl.CostEstimate(
            flops=4 * 4 * count * (keys + TEXT_PART) * 256,
            bytes_accessed=2 * 256 * (6 * count + keys),
            transcendentals=8 * count * (keys + TEXT_PART),
        ),
        name="attend_first",
    )(info, *qs, kv, text_kv)


def rest_kernel(info, q0, q1, q2, q3, kv, o_first, l_first, o_ref, keys, values, *, tile):
    count = q0.shape[0]
    blocks, size = kv.shape[:2]
    for step in range(blocks - 1):
        block = lax.rem(info[3] + step + 1, blocks)
        rows = pl.ds(step * size, size)
        keys[rows, :] = kv[block, :, :128]
        values[rows, :128] = kv[block, :, 128:]
    values[:, 128:] = jnp.ones((values.shape[0], 128), BF)
    lane = lax.broadcasted_iota(jnp.int32, (tile, 128), 1)
    for member, q_ref in enumerate((q0, q1, q2, q3)):
        target = info[4 + member]

        @pl.loop(0, count // tile)
        def _(step):
            rows = pl.ds(pl.multiple_of(step * tile, tile), tile)
            out, lse = softmax_tile(
                q_ref[rows, :].astype(F32), keys[...], values[...], None, None
            )
            before = l_first[member, rows, :]
            top = jnp.maximum(lse, before)
            new = jnp.exp2(lse - top)
            old = jnp.exp2(before - top)
            total = new + old
            o_ref[target, rows, :] = ((new * out + old * o_first[member, rows, :]) / total).astype(BF)
            rest = top + jnp.log(total) * LOG2E
            stats = jnp.zeros((tile, 128), F32)
            for part in range(3):
                piece = rest.astype(BF).astype(F32)
                stats = jnp.where(lane % HD == part, piece, stats)
                rest = rest - piece
            across = jnp.transpose(stats)
            across = jnp.concatenate([across[:8], across[HD : HD + 8]], axis=0)
            at = pl.multiple_of(count + step * STAT_ROWS, STAT_ROWS)
            o_ref[target, pl.ds(at, STAT_ROWS), :] = across.astype(BF)


def attend_rest(info, qs, kv, first):
    count = qs[0].shape[0]
    keys = (kv.shape[0] - 1) * kv.shape[1]
    tile = 128
    rows = count + count // tile * STAT_ROWS
    return pl.pallas_call(
        functools.partial(rest_kernel, tile=tile),
        out_shape=jax.ShapeDtypeStruct((4, rows, 128), BF),
        in_specs=[pl.BlockSpec(memory_space=pltpu.SMEM)] + [vmem()] * 7,
        out_specs=vmem(),
        scratch_shapes=[pltpu.VMEM((keys, 128), BF), pltpu.VMEM((keys, 256), BF)],
        compiler_params=params(20),
        cost_estimate=pl.CostEstimate(
            flops=4 * 4 * count * keys * 256,
            bytes_accessed=2 * 256 * (6 * count + keys),
            transcendentals=8 * count * keys,
        ),
        name="attend_rest",
    )(info, *qs, kv, *first)


def combine_kernel(slots, parts_ref, out):
    members = parts_ref.shape[0]
    block = 128
    count = out.shape[0] * block
    lane = lax.broadcasted_iota(jnp.int32, (block, 128), 1)
    for place in range(out.shape[0]):
        slot = slots[place]
        rows = pl.ds(pl.multiple_of(slot * block, block), block)
        at = pl.ds(pl.multiple_of(count + slot * STAT_ROWS, STAT_ROWS), STAT_ROWS)
        lses = []
        for member in range(members):
            across = parts_ref[member, at, :].astype(F32)
            across = jnp.concatenate([across, jnp.zeros((128 - STAT_ROWS, 128), F32)], axis=0)
            stats = jnp.transpose(across)
            heads = [
                stats[:, 8 * h : 8 * h + 1]
                + stats[:, 8 * h + 1 : 8 * h + 2]
                + stats[:, 8 * h + 2 : 8 * h + 3]
                for h in range(2)
            ]
            lses.append(jnp.where(lane < HD, heads[0], heads[1]))
        top = functools.reduce(jnp.maximum, lses)
        shares = [jnp.exp2(lse - top) for lse in lses]
        weighted = sum(
            share * parts_ref[member, rows, :].astype(F32) for member, share in enumerate(shares)
        )
        out[place] = (weighted / sum(shares)).astype(BF)


def combine(slots, parts):
    return pl.pallas_call(
        combine_kernel,
        out_shape=jax.ShapeDtypeStruct((4, 128, 128), BF),
        in_specs=[pl.BlockSpec(memory_space=pltpu.SMEM), vmem()],
        out_specs=vmem(),
        compiler_params=params(8),
        name="combine",
    )(slots, parts)


def share(block, axis, count):
    copies = jnp.broadcast_to(block[None], (count,) + block.shape)
    return lax.all_to_all(copies, axis, split_axis=0, concat_axis=0, tiled=True)


def on_device(latents, prompt_rows, peg_weight, modulation_weight, qkv_weight, text_len, timestep):
    frames, tile_h, tile_w, width = latents.shape[1:]
    rows_axes = ("u", "v", "zl")
    head_width = qkv_weight.shape[2]
    zl_at = lax.axis_index("zl")
    shard = qkv_weight.reshape(qkv_weight.shape[0], 3 * head_width)
    other = lax.ppermute(shard, "zl", [(0, 1), (1, 0)])
    shards = jnp.where(
        zl_at == 0, jnp.stack([shard, other]), jnp.stack([other, shard])
    ).reshape(2 * shard.shape[0], shard.shape[1])
    weight = lax.all_gather(shards, ("item", "u", "v"), axis=0, tiled=True)
    activation = jax.nn.silu(time_angles(timestep[0], modulation_weight.shape[0])).astype(BF)
    own_columns = jnp.dot(activation[None, :], modulation_weight, preferred_element_type=F32)
    modulation = share(own_columns[0], ("zh", "x"), 16).reshape(2, width)
    padded = with_halo(latents, ((rows_axes, 2), (("zh", "x"), 3)), 1)
    summed = latents.astype(F32)
    for row_tap in range(3):
        for col_tap in range(3):
            summed = summed + padded[
                :, :, row_tap : row_tap + tile_h, col_tap : col_tap + tile_w, :
            ].astype(F32) * peg_weight[row_tap, col_tap].astype(F32)
    peg = summed.astype(BF).reshape(frames * tile_h * tile_w, width)
    peg, modulation = lax.optimization_barrier((peg, modulation))
    tokens = lax.all_gather(peg, "zh", axis=0, tiled=True)
    blocks = [tokens] + [
        lax.ppermute(tokens, "x", [(i, (i + k) % 4) for i in range(4)]) for k in (1, 3, 2)
    ]
    member = lax.axis_index("v") * 2 + zl_at
    lower = member * TEXT_PART
    start = jnp.minimum(lower, prompt_rows.shape[1] - TEXT_PART)
    text_rows = lax.dynamic_slice_in_dim(prompt_rows[0], start, TEXT_PART, axis=0)
    (text_kv,) = project(text_rows, modulation, weight, (2 * head_width,))
    projected = [project(block, modulation, weight, (head_width, 2 * head_width)) for block in blocks]
    queries = jnp.concatenate([q for q, _ in projected], axis=0)
    kv = jnp.concatenate([pair for _, pair in projected], axis=0)

    swaps = (
        ("zl", [(0, 1), (1, 0)]),
        ("v", [(0, 1), (1, 0)]),
        (("v", "zl"), [(0, 3), (3, 0), (1, 2), (2, 1)]),
    )
    qs = [queries] + [lax.ppermute(queries, axis, swap) for axis, swap in swaps]
    all_kv = share(kv, "u", 4)
    info = jnp.stack(
        [start, lower, text_len[0], lax.axis_index("u")] + [member ^ k for k in range(4)]
    )
    first = attend_first(info, qs, kv, text_kv)
    parts = attend_rest(info, qs, all_kv, first)
    parts = lax.all_to_all(parts, ("v", "zl"), split_axis=0, concat_axis=0, tiled=True)
    x_at = lax.axis_index("x")
    slots = jnp.array([0, 2, 3, 1], jnp.int32)[(jnp.arange(4, dtype=jnp.int32) - x_at) % 4]
    attended = combine(slots, parts)
    attended = attended.reshape(4, 4, frames, tile_h, tile_w, head_width)
    attended = attended.transpose(2, 3, 1, 0, 4, 5)
    return attended.reshape(1, frames, tile_h, 16 * tile_w, head_width)


def solution(mesh):
    fine = Mesh(mesh.devices.reshape(2, 4, 2, 2, 4, 4), ("item", "u", "v", "zl", "zh", "x"))
    row = ("u", "v", "zl")
    col = ("zh", "x")
    in_specs = (
        P("item", None, row, col, None),
        P("item", None, None),
        P(),
        P(None, col),
        P(("item",) + row, None, col),
        P("item"),
        P("item"),
    )
    out_specs = P("item", None, row, None, col)
    return jax.shard_map(
        on_device, mesh=fine, in_specs=in_specs, out_specs=out_specs, check_vma=False
    )
```

```python
import functools
import math

import jax
import jax.numpy as jnp
from jax import lax
from jax.experimental import pallas as pl
from jax.experimental.pallas import tpu as pltpu
from jax.sharding import Mesh, PartitionSpec as P

HD = 64
LOG2E = 1.4426950408889634
SCALE2 = 0.125 * LOG2E
BF = jnp.bfloat16
F32 = jnp.float32
TEXT_PART = 64
STAT_ROWS = 16


def vmem(*shape):
    return pl.BlockSpec(memory_space=pltpu.VMEM)


def params(mib):
    return pltpu.CompilerParams(vmem_limit_bytes=mib << 20)


def with_halo(block, sides, width):
    for axis, dim in sides:
        count = lax.axis_size(axis)
        forward = [(i, i + 1) for i in range(count - 1)]
        backward = [(target, source) for source, target in forward]
        low = lax.ppermute(
            lax.slice_in_dim(block, block.shape[dim] - width, None, axis=dim), axis, forward
        )
        high = lax.ppermute(lax.slice_in_dim(block, 0, width, axis=dim), axis, backward)
        block = jnp.concatenate([low, block, high], axis=dim)
    return block


def time_angles(step, count):
    half = count // 2
    freqs = jnp.exp(-math.log(10000.0) * jnp.arange(half, dtype=F32) / half)
    angle = step.astype(F32) * freqs
    return jnp.concatenate([jnp.cos(angle), jnp.sin(angle)])


def project_kernel(slots, x0, x1, x2, x3, text, w_ref, q_out, kv_out, text_out, mod, extra):
    blocks = (x0, x1, x2, x3)
    rows = x0.shape[0]
    width = text.shape[1]
    tile = rows // 4
    for slot, block in enumerate(blocks):
        extra[slot] = block[:, width:].astype(F32)
    for place in range(4):
        for far in range(4):
            for chunk in range(3):
                at = (far * 4 + place) * 3 + chunk
                kind, first = divmod(at * 128, width)
                row = far * tile + chunk
                mod[kind : kind + 1, first : first + 128] = (
                    extra[slots[place], row : row + 1, :]
                    + extra[slots[place], row + 3 : row + 4, :]
                    + extra[slots[place], row + 6 : row + 7, :]
                )
    shift = mod[0:1, :]
    gain = 1.0 + mod[1:2, :]

    def projected(x):
        values = x.astype(F32)
        center = jnp.sum(values, axis=1, keepdims=True) * (1.0 / width)
        centered = values - center
        spread = jnp.sum(centered * centered, axis=1, keepdims=True) * (1.0 / width)
        normed = centered * lax.rsqrt(spread + 1e-06) * gain + shift
        return jnp.dot(normed.astype(BF), w_ref[...], preferred_element_type=F32).astype(BF)

    text_out[...] = projected(text[...])[:, 128:]
    for slot, block in enumerate(blocks):
        out = projected(block[:, :width])
        q_out[slot * rows : (slot + 1) * rows, :] = out[:, :128]
        kv_out[slot * rows : (slot + 1) * rows, :] = out[:, 128:]


def project(slots, blocks, text, weight):
    rows, lanes = blocks[0].shape
    width = text.shape[1]
    return pl.pallas_call(
        project_kernel,
        out_shape=[
            jax.ShapeDtypeStruct((4 * rows, 128), BF),
            jax.ShapeDtypeStruct((4 * rows, 256), BF),
            jax.ShapeDtypeStruct((text.shape[0], 256), BF),
        ],
        in_specs=[pl.BlockSpec(memory_space=pltpu.SMEM)] + [vmem()] * 6,
        out_specs=[vmem()] * 3,
        scratch_shapes=[pltpu.VMEM((2, width), F32), pltpu.VMEM((4, rows, 128), F32)],
        compiler_params=params(20),
        cost_estimate=pl.CostEstimate(
            flops=8 * rows * width * weight.shape[1],
            bytes_accessed=2 * (4 * rows * lanes + weight.size),
            transcendentals=4 * rows,
        ),
        name="project",
    )(slots, *blocks, text, weight)


def softmax_tile(q, keys, values, text, valid):
    contract = (((1,), (1,)), ((), ()))
    lane = lax.broadcasted_iota(jnp.int32, (q.shape[0], 128), 1)
    outs, sums = [], []
    for head in range(2):
        own = jnp.where(lane // HD == head, q, 0.0).astype(BF)
        s = lax.dot_general(own, keys, contract, preferred_element_type=F32)
        top = jnp.max(s, axis=1, keepdims=True)
        if text is not None:
            t = lax.dot_general(own, text[0], contract, preferred_element_type=F32)
            t = jnp.where(valid, t, -1e30)
            top = jnp.maximum(top, jnp.max(t, axis=1, keepdims=True))
        top = top * SCALE2
        p = jnp.exp2(s * SCALE2 - top).astype(BF)
        acc = jnp.dot(p, values, preferred_element_type=F32)
        if text is not None:
            pt = jnp.where(valid, jnp.exp2(t * SCALE2 - top), 0.0).astype(BF)
            acc = acc + jnp.dot(pt, text[1], preferred_element_type=F32)
        total = acc[:, 128:]
        outs.append(acc[:, :128] / total)
        sums.append(top + jnp.log(total) * LOG2E)
    return jnp.where(lane < HD, outs[0], outs[1]), jnp.where(lane < HD, sums[0], sums[1])


def attend_kernel(info, q_ref, kv, text_kv, o_ref, values, text_values, *, tile):
    members, count = q_ref.shape[:2]
    values[:, :128] = kv[:, 128:]
    values[:, 128:] = jnp.ones((kv.shape[0], 128), BF)
    text_values[:, :128] = text_kv[:, 128:]
    text_values[:, 128:] = jnp.ones((TEXT_PART, 128), BF)
    lane = lax.broadcasted_iota(jnp.int32, (tile, 128), 1)
    position = info[0] + lax.broadcasted_iota(jnp.int32, (tile, TEXT_PART), 1)
    valid = (position >= info[1]) & (position < info[2])
    for member in range(members):

        @pl.loop(0, count // tile)
        def _(step):
            rows = pl.ds(pl.multiple_of(step * tile, tile), tile)
            out, rest = softmax_tile(
                q_ref[member, rows, :].astype(F32),
                kv[:, :128],
                values[...],
                (text_kv[:, :128], text_values[...]),
                valid,
            )
            o_ref[member, rows, :] = out.astype(BF)
            stats = jnp.zeros((tile, 128), F32)
            for part in range(3):
                piece = rest.astype(BF).astype(F32)
                stats = jnp.where(lane % HD == part, piece, stats)
                rest = rest - piece
            across = jnp.transpose(stats)
            across = jnp.concatenate([across[:8], across[HD : HD + 8]], axis=0)
            at = pl.multiple_of(count + step * STAT_ROWS, STAT_ROWS)
            o_ref[member, pl.ds(at, STAT_ROWS), :] = across.astype(BF)


def attend(info, qs, kv, text_kv):
    members, count = qs.shape[:2]
    keys = kv.shape[0]
    tile = 128
    rows = count + count // tile * STAT_ROWS
    return pl.pallas_call(
        functools.partial(attend_kernel, tile=tile),
        out_shape=jax.ShapeDtypeStruct((members, rows, 128), BF),
        in_specs=[pl.BlockSpec(memory_space=pltpu.SMEM)] + [vmem()] * 3,
        out_specs=vmem(),
        scratch_shapes=[pltpu.VMEM((keys, 256), BF), pltpu.VMEM((TEXT_PART, 256), BF)],
        compiler_params=params(24),
        cost_estimate=pl.CostEstimate(
            flops=4 * 4 * count * (keys + TEXT_PART) * 256,
            bytes_accessed=2 * 256 * (6 * count + keys),
            transcendentals=8 * count * (keys + TEXT_PART),
        ),
        name="attend",
    )(info, qs, kv, text_kv)


def combine_kernel(slots, parts_ref, out):
    members = parts_ref.shape[0]
    block = 128
    count = out.shape[0] * block
    lane = lax.broadcasted_iota(jnp.int32, (block, 128), 1)
    for place in range(out.shape[0]):
        slot = slots[place]
        rows = pl.ds(pl.multiple_of(slot * block, block), block)
        at = pl.ds(pl.multiple_of(count + slot * STAT_ROWS, STAT_ROWS), STAT_ROWS)
        lses = []
        for member in range(members):
            across = parts_ref[member, at, :].astype(F32)
            across = jnp.concatenate([across, jnp.zeros((128 - STAT_ROWS, 128), F32)], axis=0)
            stats = jnp.transpose(across)
            heads = [
                stats[:, 8 * h : 8 * h + 1]
                + stats[:, 8 * h + 1 : 8 * h + 2]
                + stats[:, 8 * h + 2 : 8 * h + 3]
                for h in range(2)
            ]
            lses.append(jnp.where(lane < HD, heads[0], heads[1]))
        top = functools.reduce(jnp.maximum, lses)
        shares = [jnp.exp2(lse - top) for lse in lses]
        weighted = sum(
            share * parts_ref[member, rows, :].astype(F32) for member, share in enumerate(shares)
        )
        out[place] = (weighted / sum(shares)).astype(BF)


def combine(slots, parts):
    return pl.pallas_call(
        combine_kernel,
        out_shape=jax.ShapeDtypeStruct((4, 128, 128), BF),
        in_specs=[pl.BlockSpec(memory_space=pltpu.SMEM), vmem()],
        out_specs=vmem(),
        compiler_params=params(8),
        name="combine",
    )(slots, parts)


def share(block, axis, count):
    copies = jnp.broadcast_to(block[None], (count,) + block.shape)
    return lax.all_to_all(copies, axis, split_axis=0, concat_axis=0, tiled=True)


def on_device(latents, prompt_rows, peg_weight, modulation_weight, qkv_weight, text_len, timestep):
    frames, tile_h, tile_w, width = latents.shape[1:]
    head_width = qkv_weight.shape[2]
    zl_at = lax.axis_index("zl")
    x_at = lax.axis_index("x")
    member = lax.axis_index("v") * 2 + zl_at

    rows = with_halo(latents, ((("u", "v", "zl"), 2),), 1)
    shard = qkv_weight.reshape(qkv_weight.shape[0], 3 * head_width)
    rows, shard = lax.optimization_barrier((rows, shard))
    other = lax.ppermute(shard, "zl", [(0, 1), (1, 0)])
    shards = jnp.where(
        zl_at == 0, jnp.stack([shard, other]), jnp.stack([other, shard])
    ).reshape(2 * shard.shape[0], shard.shape[1])
    weight = lax.all_gather(shards, ("item", "u", "v"), axis=0, tiled=True)
    padded = with_halo(rows, ((("zh", "x"), 3),), 1)
    summed = latents.astype(F32)
    for row_tap in range(3):
        for col_tap in range(3):
            summed = summed + padded[
                :, :, row_tap : row_tap + tile_h, col_tap : col_tap + tile_w, :
            ].astype(F32) * peg_weight[row_tap, col_tap].astype(F32)
    peg = summed.astype(BF).reshape(frames * tile_h * tile_w, width)

    activation = jax.nn.silu(time_angles(timestep[0], modulation_weight.shape[0])).astype(BF)
    own_columns = jnp.dot(activation[None, :], modulation_weight, preferred_element_type=F32)
    rest = own_columns.reshape(3, 128)
    pieces = []
    for _ in range(3):
        pieces.append(lax.reduce_precision(rest, 8, 7))
        rest = rest - pieces[-1]
    extra = jnp.concatenate(pieces).astype(BF)
    extra = jnp.pad(extra, ((0, peg.shape[0] - 9), (0, 0)))
    peg = jnp.concatenate([peg, extra], axis=1)

    tokens = lax.all_gather(peg, "zh", axis=0, tiled=True)
    blocks = [tokens] + [
        lax.ppermute(tokens, "x", [(i, (i + k) % 4) for i in range(4)]) for k in (1, 3, 2)
    ]
    distance = (jnp.arange(4, dtype=jnp.int32) - x_at) % 4
    slots = jnp.where(distance == 0, 0, jnp.where(distance == 3, 1, distance + 1))

    lower = member * TEXT_PART
    start = jnp.minimum(lower, prompt_rows.shape[1] - TEXT_PART)
    text_rows = lax.dynamic_slice_in_dim(prompt_rows[0], start, TEXT_PART, axis=0)
    queries, kv, text_kv = project(slots, blocks, text_rows, weight)

    all_kv = lax.all_gather(kv, "u", axis=0, tiled=True)
    qs = share(queries, ("v", "zl"), 4)
    info = jnp.stack([start, lower, text_len[0]])
    parts = attend(info, qs, all_kv, text_kv)
    parts = lax.all_to_all(parts, ("v", "zl"), split_axis=0, concat_axis=0, tiled=True)
    attended = combine(slots, parts)
    attended = attended.reshape(4, 4, frames, tile_h, tile_w, head_width)
    attended = attended.transpose(2, 3, 1, 0, 4, 5)
    return attended.reshape(1, frames, tile_h, 16 * tile_w, head_width)


def solution(mesh):
    fine = Mesh(mesh.devices.reshape(2, 4, 2, 2, 4, 4), ("item", "u", "v", "zl", "zh", "x"))
    row = ("u", "v", "zl")
    col = ("zh", "x")
    in_specs = (
        P("item", None, row, col, None),
        P("item", None, None),
        P(),
        P(None, col),
        P(("item",) + row, None, col),
        P("item"),
        P("item"),
    )
    out_specs = P("item", None, row, None, col)
    return jax.shard_map(
        on_device, mesh=fine, in_specs=in_specs, out_specs=out_specs, check_vma=False
    )
```

```python
import functools
import math

import jax
import jax.numpy as jnp
from jax import lax
from jax.experimental import pallas as pl
from jax.experimental.pallas import tpu as pltpu
from jax.sharding import Mesh, PartitionSpec as P

HD = 64
LOG2E = 1.4426950408889634
SCALE2 = 0.125 * LOG2E
BF = jnp.bfloat16
F32 = jnp.float32
TEXT_PART = 64
STAT_ROWS = 16


def vmem(*shape):
    return pl.BlockSpec(memory_space=pltpu.VMEM)


def params(mib):
    return pltpu.CompilerParams(vmem_limit_bytes=mib << 20)


def with_halo(block, sides, width):
    for axis, dim in sides:
        count = lax.axis_size(axis)
        forward = [(i, i + 1) for i in range(count - 1)]
        backward = [(target, source) for source, target in forward]
        low = lax.ppermute(
            lax.slice_in_dim(block, block.shape[dim] - width, None, axis=dim), axis, forward
        )
        high = lax.ppermute(lax.slice_in_dim(block, 0, width, axis=dim), axis, backward)
        block = jnp.concatenate([low, block, high], axis=dim)
    return block


def time_angles(step, count):
    half = count // 2
    freqs = jnp.exp(-math.log(10000.0) * jnp.arange(half, dtype=F32) / half)
    angle = step.astype(F32) * freqs
    return jnp.concatenate([jnp.cos(angle), jnp.sin(angle)])


def project_kernel(
    slots, x0, x1, x2, x3, text, w_ref, q_out, text_out, q_copies, kv_copies, mod, extra, kv_out, sems
):
    blocks = (x0, x1, x2, x3)
    rows = x0.shape[0]
    width = text.shape[1]
    tile = rows // 4
    for slot, block in enumerate(blocks):
        extra[slot] = block[:, width:].astype(F32)
    for place in range(4):
        for far in range(4):
            for chunk in range(3):
                at = (far * 4 + place) * 3 + chunk
                kind, first = divmod(at * 128, width)
                row = far * tile + chunk
                mod[kind : kind + 1, first : first + 128] = (
                    extra[slots[place], row : row + 1, :]
                    + extra[slots[place], row + 3 : row + 4, :]
                    + extra[slots[place], row + 6 : row + 7, :]
                )
    shift = mod[0:1, :]
    gain = 1.0 + mod[1:2, :]

    def projected(x):
        values = x.astype(F32)
        center = jnp.sum(values, axis=1, keepdims=True) * (1.0 / width)
        centered = values - center
        spread = jnp.sum(centered * centered, axis=1, keepdims=True) * (1.0 / width)
        normed = centered * lax.rsqrt(spread + 1e-06) * gain + shift
        return jnp.dot(normed.astype(BF), w_ref[...], preferred_element_type=F32).astype(BF)

    text_out[...] = projected(text[...])[:, 128:]
    for slot, block in enumerate(blocks):
        out = projected(block[:, :width])
        q_out[slot * rows : (slot + 1) * rows, :] = out[:, :128]
        kv_out[slot * rows : (slot + 1) * rows, :] = out[:, 128:]
    copies = [
        pltpu.make_async_copy(block, copies.at[i], sems.at[kind, i])
        for kind, (block, copies) in enumerate(((q_out, q_copies), (kv_out, kv_copies)))
        for i in range(4)
    ]
    for copy in copies:
        copy.start()
    for copy in copies:
        copy.wait()


def project(slots, blocks, text, weight):
    rows, lanes = blocks[0].shape
    width = text.shape[1]
    return pl.pallas_call(
        project_kernel,
        out_shape=[
            jax.ShapeDtypeStruct((4 * rows, 128), BF),
            jax.ShapeDtypeStruct((text.shape[0], 256), BF),
            jax.ShapeDtypeStruct((4, 4 * rows, 128), BF),
            jax.ShapeDtypeStruct((4, 4 * rows, 256), BF),
        ],
        in_specs=[pl.BlockSpec(memory_space=pltpu.SMEM)] + [vmem()] * 6,
        out_specs=[vmem()] * 2 + [pl.BlockSpec(memory_space=pl.ANY)] * 2,
        scratch_shapes=[
            pltpu.VMEM((2, width), F32),
            pltpu.VMEM((4, rows, 128), F32),
            pltpu.VMEM((4 * rows, 256), BF),
            pltpu.SemaphoreType.DMA((2, 4)),
        ],
        compiler_params=params(20),
        cost_estimate=pl.CostEstimate(
            flops=8 * rows * width * weight.shape[1],
            bytes_accessed=2 * (4 * rows * lanes + weight.size),
            transcendentals=4 * rows,
        ),
        name="project",
    )(slots, *blocks, text, weight)


def load_keys(kv, text_kv, keys, values):
    blocks, size = kv.shape[:2]
    for block in range(blocks):
        rows = pl.ds(block * size, size)
        keys[rows, :] = kv[block, :, :128]
        values[rows, :128] = kv[block, :, 128:]
    at = blocks * size
    pad = 128 - TEXT_PART
    keys[at : at + TEXT_PART, :] = text_kv[:, :128]
    keys[at + TEXT_PART :, :] = jnp.zeros((pad, 128), BF)
    values[at : at + TEXT_PART, :128] = text_kv[:, 128:]
    values[at + TEXT_PART :, :128] = jnp.zeros((pad, 128), BF)
    values[:, 128:] = jnp.ones((values.shape[0], 128), BF)


def softmax_block(info, q, keys, values):
    rows = q.shape[0]
    latent = keys.shape[0] - 128
    lane = lax.broadcasted_iota(jnp.int32, (rows, 128), 1)
    position = info[0] + lane
    valid = (position >= info[1]) & (position < info[2]) & (lane < TEXT_PART)
    q = q.astype(F32)
    outs, sums = [], []
    for head in range(2):
        own = jnp.where(lane // HD == head, q, 0.0).astype(BF)
        s = lax.dot_general(
            own, keys[...], (((1,), (1,)), ((), ())), preferred_element_type=F32
        )
        text = jnp.where(valid, s[:, latent:], -1e30)
        top = jnp.maximum(
            jnp.max(s[:, :latent], axis=1, keepdims=True), jnp.max(text, axis=1, keepdims=True)
        )
        top = top * SCALE2
        p = jnp.exp2(s[:, :latent] * SCALE2 - top).astype(BF)
        p_text = jnp.where(valid, jnp.exp2(text * SCALE2 - top), 0.0).astype(BF)
        p = jnp.concatenate([p, p_text], axis=1)
        acc = jnp.dot(p, values[...], preferred_element_type=F32)
        total = acc[:, 128:]
        outs.append(acc[:, :128] / total)
        sums.append(top + jnp.log(total) * LOG2E)
    return jnp.where(lane < HD, outs[0], outs[1]), jnp.where(lane < HD, sums[0], sums[1])


def peers_kernel(info, q_ref, kv, text_kv, o_ref, keys, values):
    members, count = q_ref.shape[:2]
    load_keys(kv, text_kv, keys, values)
    lane = lax.broadcasted_iota(jnp.int32, (128, 128), 1)

    @pl.loop(1, members)
    def _(step):
        member = jnp.bitwise_xor(info[3], step)
        out, lse = softmax_block(info, q_ref[member], keys, values)
        o_ref[member, :count, :] = out.astype(BF)
        for tile in range(count // 128):
            rest = lse[tile * 128 : (tile + 1) * 128]
            stats = jnp.zeros((128, 128), F32)
            for part in range(3):
                piece = rest.astype(BF).astype(F32)
                stats = jnp.where(lane % HD == part, piece, stats)
                rest = rest - piece
            across = jnp.transpose(stats)
            across = jnp.concatenate([across[:8], across[HD : HD + 8]], axis=0)
            at = count + tile * STAT_ROWS
            o_ref[member, at : at + STAT_ROWS, :] = across.astype(BF)


def own_kernel(info, q_ref, kv, text_kv, o_ref, l_ref, keys, values):
    load_keys(kv, text_kv, keys, values)
    out, lse = softmax_block(info, q_ref[...], keys, values)
    o_ref[...] = out
    l_ref[...] = lse


def attend(kernel, name, blocks, out_shape, info, q, kv, text_kv):
    keys = kv.shape[0] * kv.shape[1] + 128
    count = q.shape[-2]
    return pl.pallas_call(
        kernel,
        out_shape=out_shape,
        in_specs=[pl.BlockSpec(memory_space=pltpu.SMEM)] + [vmem()] * 3,
        out_specs=jax.tree.map(lambda _: vmem(), out_shape),
        scratch_shapes=[pltpu.VMEM((keys, 128), BF), pltpu.VMEM((keys, 256), BF)],
        compiler_params=params(32),
        cost_estimate=pl.CostEstimate(
            flops=4 * blocks * count * keys * 256,
            bytes_accessed=2 * (q.size + kv.size),
            transcendentals=2 * blocks * count * keys,
        ),
        name=name,
    )(info, q, kv, text_kv)


def combine_kernel(slots, info, parts_ref, o_ref, l_ref, out):
    members = parts_ref.shape[0]
    block = 128
    count = o_ref.shape[0]
    lane = lax.broadcasted_iota(jnp.int32, (block, 128), 1)
    for place in range(out.shape[0]):
        slot = slots[place]
        rows = pl.ds(pl.multiple_of(slot * block, block), block)
        at = pl.ds(pl.multiple_of(count + slot * STAT_ROWS, STAT_ROWS), STAT_ROWS)
        lses = [l_ref[rows, :]]
        outs = [o_ref[rows, :]]
        for step in range(1, members):
            member = jnp.bitwise_xor(info[3], step)
            across = parts_ref[member, at, :].astype(F32)
            across = jnp.concatenate([across, jnp.zeros((128 - STAT_ROWS, 128), F32)], axis=0)
            stats = jnp.transpose(across)
            heads = [
                stats[:, 8 * h : 8 * h + 1]
                + stats[:, 8 * h + 1 : 8 * h + 2]
                + stats[:, 8 * h + 2 : 8 * h + 3]
                for h in range(2)
            ]
            lses.append(jnp.where(lane < HD, heads[0], heads[1]))
            outs.append(parts_ref[member, rows, :].astype(F32))
        top = functools.reduce(jnp.maximum, lses)
        shares = [jnp.exp2(lse - top) for lse in lses]
        weighted = sum(share * part for share, part in zip(shares, outs))
        out[place] = (weighted / sum(shares)).astype(BF)


def combine(slots, info, parts, own):
    smem = pl.BlockSpec(memory_space=pltpu.SMEM)
    return pl.pallas_call(
        combine_kernel,
        out_shape=jax.ShapeDtypeStruct((4, 128, 128), BF),
        in_specs=[smem, smem] + [vmem()] * 3,
        out_specs=vmem(),
        compiler_params=params(8),
        name="combine",
    )(slots, info, parts, *own)


def on_device(latents, prompt_rows, peg_weight, modulation_weight, qkv_weight, text_len, timestep):
    frames, tile_h, tile_w, width = latents.shape[1:]
    head_width = qkv_weight.shape[2]
    zl_at = lax.axis_index("zl")
    x_at = lax.axis_index("x")
    member = lax.axis_index("v") * 2 + zl_at

    shard = qkv_weight.reshape(qkv_weight.shape[0], 3 * head_width)
    half = lax.all_gather(shard, ("item", "u", "v"), axis=0, tiled=True)
    padded = with_halo(latents, ((("u", "v", "zl"), 2), (("zh", "x"), 3)), 1)
    summed = latents.astype(F32)
    for row_tap in range(3):
        for col_tap in range(3):
            summed = summed + padded[
                :, :, row_tap : row_tap + tile_h, col_tap : col_tap + tile_w, :
            ].astype(F32) * peg_weight[row_tap, col_tap].astype(F32)
    peg = summed.astype(BF).reshape(frames * tile_h * tile_w, width)

    activation = jax.nn.silu(time_angles(timestep[0], modulation_weight.shape[0])).astype(BF)
    own_columns = jnp.dot(activation[None, :], modulation_weight, preferred_element_type=F32)
    rest = own_columns.reshape(3, 128)
    pieces = []
    for _ in range(3):
        pieces.append(lax.reduce_precision(rest, 8, 7))
        rest = rest - pieces[-1]
    extra = jnp.concatenate(pieces).astype(BF)
    extra = jnp.pad(extra, ((0, peg.shape[0] - 9), (0, 0)))
    peg = jnp.concatenate([peg, extra], axis=1)

    tokens = lax.all_gather(peg, "zh", axis=0, tiled=True)
    tokens, half = lax.optimization_barrier((tokens, half))
    blocks = [tokens] + [
        lax.ppermute(tokens, "x", [(i, (i + k) % 4) for i in range(4)]) for k in (1, 3, 2)
    ]
    other = lax.ppermute(half, "zl", [(0, 1), (1, 0)])
    pieces = (-1, shard.shape[0], shard.shape[1])
    half, other = half.reshape(pieces), other.reshape(pieces)
    weight = jnp.where(
        zl_at == 0, jnp.stack([half, other], axis=1), jnp.stack([other, half], axis=1)
    ).reshape(width, 3 * head_width)
    distance = (jnp.arange(4, dtype=jnp.int32) - x_at) % 4
    slots = jnp.where(distance == 0, 0, jnp.where(distance == 3, 1, distance + 1))

    lower = member * TEXT_PART
    start = jnp.minimum(lower, prompt_rows.shape[1] - TEXT_PART)
    text_rows = lax.dynamic_slice_in_dim(prompt_rows[0], start, TEXT_PART, axis=0)
    queries, text_kv, q_copies, kv_copies = project(slots, blocks, text_rows, weight)
    group = ("v", "zl")
    qs = lax.all_to_all(q_copies, group, split_axis=0, concat_axis=0, tiled=True)
    kv = lax.all_to_all(kv_copies, "u", split_axis=0, concat_axis=0, tiled=True)
    info = jnp.stack([start, lower, text_len[0], member])
    count = queries.shape[0]
    part = jax.ShapeDtypeStruct((4, count + count // 128 * STAT_ROWS, 128), BF)
    parts = attend(peers_kernel, "peers", 3, part, info, qs, kv, text_kv)
    parts = lax.all_to_all(parts, group, split_axis=0, concat_axis=0, tiled=True)
    plain = jax.ShapeDtypeStruct((count, 128), F32)
    own = attend(own_kernel, "own", 1, [plain, plain], info, queries, kv, text_kv)
    attended = combine(slots, info, parts, own)
    attended = attended.reshape(4, 4, frames, tile_h, tile_w, head_width)
    attended = attended.transpose(2, 3, 1, 0, 4, 5)
    return attended.reshape(1, frames, tile_h, 16 * tile_w, head_width)


def solution(mesh):
    fine = Mesh(mesh.devices.reshape(2, 4, 2, 2, 4, 4), ("item", "u", "v", "zl", "zh", "x"))
    row = ("u", "v", "zl")
    col = ("zh", "x")
    in_specs = (
        P("item", None, row, col, None),
        P("item", None, None),
        P(),
        P(None, col),
        P(("item",) + row, None, col),
        P("item"),
        P("item"),
    )
    out_specs = P("item", None, row, None, col)
    return jax.shard_map(
        on_device, mesh=fine, in_specs=in_specs, out_specs=out_specs, check_vma=False
    )
```

```python
import functools
import math

import jax
import jax.numpy as jnp
from jax import lax
from jax.experimental import pallas as pl
from jax.experimental.pallas import tpu as pltpu
from jax.sharding import Mesh, PartitionSpec as P

HD = 64
LOG2E = 1.4426950408889634
SCALE2 = 0.125 * LOG2E
BF = jnp.bfloat16
F32 = jnp.float32
TEXT_PART = 64
STAT_ROWS = 16


def vmem(*shape):
    return pl.BlockSpec(memory_space=pltpu.VMEM)


def hbm():
    return pl.BlockSpec(memory_space=pltpu.MemorySpace.HBM)


def keep(x):
    return pltpu.with_memory_space_constraint(x, pltpu.MemorySpace.HBM)


def params(mib):
    return pltpu.CompilerParams(vmem_limit_bytes=mib << 20)


def with_halo(block, sides, width):
    for axis, dim in sides:
        count = lax.axis_size(axis)
        forward = [(i, i + 1) for i in range(count - 1)]
        backward = [(target, source) for source, target in forward]
        low = lax.ppermute(
            lax.slice_in_dim(block, block.shape[dim] - width, None, axis=dim), axis, forward
        )
        high = lax.ppermute(lax.slice_in_dim(block, 0, width, axis=dim), axis, backward)
        block = jnp.concatenate([low, block, high], axis=dim)
    return block


def time_angles(step, count):
    half = count // 2
    freqs = jnp.exp(-math.log(10000.0) * jnp.arange(half, dtype=F32) / half)
    angle = step.astype(F32) * freqs
    return jnp.concatenate([jnp.cos(angle), jnp.sin(angle)])


def project_kernel(
    slots, x0, a0, a1, b0, b1, c0, c1, text, w_hbm,
    text_out, q_copies, kv_copies,
    held, mod, extra, normed, w_ref, q_out, kv_out, sems, in_sems, w_sem,
):
    rows = x0.shape[0]
    half = rows // 2
    width = text.shape[1]
    tile = rows // 4
    arrived = [(x0, 0)]
    for slot, (low, high) in enumerate(((a0, a1), (b0, b1), (c0, c1))):
        arrived += [(low, (slot + 1) * rows), (high, (slot + 1) * rows + half)]
    fetches = []
    for i, (piece, at) in enumerate(arrived):
        fetches.append(
            pltpu.make_async_copy(piece, held.at[pl.ds(at, piece.shape[0]), :], in_sems.at[i])
        )
        fetches[-1].start()
    fetch = pltpu.make_async_copy(w_hbm, w_ref, w_sem)
    fetch.start()
    for copy in fetches:
        copy.wait()
    for slot in range(4):
        extra[slot] = held[slot * rows : (slot + 1) * rows, width:].astype(F32)
    for place in range(4):
        for far in range(4):
            for chunk in range(3):
                at = (far * 4 + place) * 3 + chunk
                kind, first = divmod(at * 128, width)
                row = far * tile + chunk
                mod[kind : kind + 1, first : first + 128] = (
                    extra[slots[place], row : row + 1, :]
                    + extra[slots[place], row + 3 : row + 4, :]
                    + extra[slots[place], row + 6 : row + 7, :]
                )
    shift = mod[0:1, :]
    gain = 1.0 + mod[1:2, :]
    for block in range(5):
        at = block * rows
        count = rows if block < 4 else text.shape[0]
        values = (held[at : at + rows, :width] if block < 4 else text[...]).astype(F32)
        center = jnp.sum(values, axis=1, keepdims=True) * (1.0 / width)
        centered = values - center
        spread = jnp.sum(centered * centered, axis=1, keepdims=True) * (1.0 / width)
        result = centered * lax.rsqrt(spread + 1e-06) * gain + shift
        normed[at : at + count, :] = result.astype(BF)
    fetch.wait()
    out = jnp.dot(normed[...], w_ref[...], preferred_element_type=F32).astype(BF)
    q_out[...] = out[: 4 * rows, :128]
    kv_out[...] = out[: 4 * rows, 128:]
    text_out[...] = out[4 * rows :, 128:]
    copies = [
        pltpu.make_async_copy(block, copies.at[i], sems.at[kind, i])
        for kind, (block, copies) in enumerate(((q_out, q_copies), (kv_out, kv_copies)))
        for i in range(4)
    ]
    for copy in copies:
        copy.start()
    for copy in copies:
        copy.wait()


def project(slots, pieces, text, weight):
    rows, lanes = pieces[0].shape
    width = text.shape[1]
    return pl.pallas_call(
        project_kernel,
        out_shape=[
            jax.ShapeDtypeStruct((text.shape[0], 256), BF),
            pltpu.MemorySpace.HBM((4, 4 * rows, 128), BF),
            pltpu.MemorySpace.HBM((4, 4 * rows, 256), BF),
        ],
        in_specs=[pl.BlockSpec(memory_space=pltpu.SMEM)] + [hbm()] * 7 + [vmem(), hbm()],
        out_specs=[vmem()] + [hbm()] * 2,
        scratch_shapes=[
            pltpu.VMEM((4 * rows, lanes), BF),
            pltpu.VMEM((2, width), F32),
            pltpu.VMEM((4, rows, 128), F32),
            pltpu.VMEM((4 * rows + text.shape[0], width), BF),
            pltpu.VMEM(weight.shape, BF),
            pltpu.VMEM((4 * rows, 128), BF),
            pltpu.VMEM((4 * rows, 256), BF),
            pltpu.SemaphoreType.DMA((2, 4)),
            pltpu.SemaphoreType.DMA((7,)),
            pltpu.SemaphoreType.DMA,
        ],
        compiler_params=params(28),
        cost_estimate=pl.CostEstimate(
            flops=8 * rows * width * weight.shape[1],
            bytes_accessed=2 * (4 * rows * lanes + weight.size),
            transcendentals=4 * rows,
        ),
        name="project",
    )(slots, *map(keep, pieces), text, keep(weight))


def load_keys(kv, text_kv, keys, values):
    blocks, size = kv.shape[:2]
    for block in range(blocks):
        rows = pl.ds(block * size, size)
        keys[rows, :] = kv[block, :, :128]
        values[rows, :128] = kv[block, :, 128:]
    at = blocks * size
    pad = 128 - TEXT_PART
    keys[at : at + TEXT_PART, :] = text_kv[:, :128]
    keys[at + TEXT_PART :, :] = jnp.zeros((pad, 128), BF)
    values[at : at + TEXT_PART, :128] = text_kv[:, 128:]
    values[at + TEXT_PART :, :128] = jnp.zeros((pad, 128), BF)
    values[:, 128:] = jnp.ones((values.shape[0], 128), BF)


def softmax_block(info, q, keys, values):
    rows = q.shape[0]
    latent = keys.shape[0] - 128
    lane = lax.broadcasted_iota(jnp.int32, (rows, 128), 1)
    position = info[0] + lane
    valid = (position >= info[1]) & (position < info[2]) & (lane < TEXT_PART)
    q = q.astype(F32)
    outs, sums = [], []
    for head in range(2):
        own = jnp.where(lane // HD == head, q, 0.0).astype(BF)
        s = lax.dot_general(
            own, keys[...], (((1,), (1,)), ((), ())), preferred_element_type=F32
        )
        text = jnp.where(valid, s[:, latent:], -1e30)
        top = jnp.maximum(
            jnp.max(s[:, :latent], axis=1, keepdims=True), jnp.max(text, axis=1, keepdims=True)
        )
        top = top * SCALE2
        p = jnp.exp2(s[:, :latent] * SCALE2 - top).astype(BF)
        p_text = jnp.where(valid, jnp.exp2(text * SCALE2 - top), 0.0).astype(BF)
        p = jnp.concatenate([p, p_text], axis=1)
        acc = jnp.dot(p, values[...], preferred_element_type=F32)
        total = acc[:, 128:]
        outs.append(acc[:, :128] / total)
        sums.append(top + jnp.log(total) * LOG2E)
    return jnp.where(lane < HD, outs[0], outs[1]), jnp.where(lane < HD, sums[0], sums[1])


def peers_kernel(info, q_ref, kv, text_kv, o_ref, keys, values, held, sems):
    members, count = q_ref.shape[:2]
    load_keys(kv, text_kv, keys, values)
    lane = lax.broadcasted_iota(jnp.int32, (128, 128), 1)

    def send(step):
        member = jnp.bitwise_xor(info[3], step)
        return pltpu.make_async_copy(held.at[step], o_ref.at[member], sems.at[step])

    @pl.loop(1, members)
    def _(step):
        out, lse = softmax_block(info, q_ref[jnp.bitwise_xor(info[3], step)], keys, values)
        held[step, :count, :] = out.astype(BF)
        for tile in range(count // 128):
            rest = lse[tile * 128 : (tile + 1) * 128]
            stats = jnp.zeros((128, 128), F32)
            for part in range(3):
                piece = rest.astype(BF).astype(F32)
                stats = jnp.where(lane % HD == part, piece, stats)
                rest = rest - piece
            across = jnp.transpose(stats)
            across = jnp.concatenate([across[:8], across[HD : HD + 8]], axis=0)
            at = count + tile * STAT_ROWS
            held[step, at : at + STAT_ROWS, :] = across.astype(BF)
        send(step).start()

    for step in range(1, members):
        send(step).wait()


def own_kernel(info, q_ref, kv, text_kv, o_ref, keys, values, held, sems):
    load_keys(kv, text_kv, keys, values)
    out, lse = softmax_block(info, q_ref[info[3]], keys, values)
    held[0] = out
    held[1] = lse
    copy = pltpu.make_async_copy(held, o_ref, sems.at[0])
    copy.start()
    copy.wait()


def attend(kernel, name, blocks, out_shape, info, q, kv, text_kv):
    keys = kv.shape[0] * kv.shape[1] + 128
    count = q.shape[-2]
    return pl.pallas_call(
        kernel,
        out_shape=pltpu.MemorySpace.HBM(out_shape.shape, out_shape.dtype),
        in_specs=[pl.BlockSpec(memory_space=pltpu.SMEM)] + [vmem()] * 3,
        out_specs=hbm(),
        scratch_shapes=[
            pltpu.VMEM((keys, 128), BF),
            pltpu.VMEM((keys, 256), BF),
            pltpu.VMEM(out_shape.shape, out_shape.dtype),
            pltpu.SemaphoreType.DMA((4,)),
        ],
        compiler_params=params(24),
        cost_estimate=pl.CostEstimate(
            flops=4 * blocks * count * keys * 256,
            bytes_accessed=2 * (q.size + kv.size),
            transcendentals=2 * blocks * count * keys,
        ),
        name=name,
    )(info, q, kv, text_kv)


def combine_kernel(slots, info, parts_ref, own_hbm, out, grid, own, sem):
    copy = pltpu.make_async_copy(own_hbm, own, sem)
    copy.start()
    copy.wait()
    o_ref, l_ref = own.at[0], own.at[1]
    members = parts_ref.shape[0]
    block = 128
    count = o_ref.shape[0]
    lane = lax.broadcasted_iota(jnp.int32, (block, 128), 1)
    frames, tile_h, cells = out.shape[:3]
    tile_w = cells // 16
    for place in range(4):
        slot = slots[place]
        rows = pl.ds(pl.multiple_of(slot * block, block), block)
        at = pl.ds(pl.multiple_of(count + slot * STAT_ROWS, STAT_ROWS), STAT_ROWS)
        lses = [l_ref[rows, :]]
        outs = [o_ref[rows, :]]
        for step in range(1, members):
            member = jnp.bitwise_xor(info[3], step)
            across = parts_ref[member, at, :].astype(F32)
            across = jnp.concatenate([across, jnp.zeros((128 - STAT_ROWS, 128), F32)], axis=0)
            stats = jnp.transpose(across)
            heads = [
                stats[:, 8 * h : 8 * h + 1]
                + stats[:, 8 * h + 1 : 8 * h + 2]
                + stats[:, 8 * h + 2 : 8 * h + 3]
                for h in range(2)
            ]
            lses.append(jnp.where(lane < HD, heads[0], heads[1]))
            outs.append(parts_ref[member, rows, :].astype(F32))
        top = functools.reduce(jnp.maximum, lses)
        shares = [jnp.exp2(lse - top) for lse in lses]
        weighted = sum(share * part for share, part in zip(shares, outs))
        merged = weighted / sum(shares)
        at = 0
        for far in range(4):
            for frame in range(frames):
                for row in range(tile_h):
                    first = (far * 4 + place) * tile_w
                    grid[frame, row, first : first + tile_w, :] = merged[at : at + tile_w]
                    at += tile_w
    out[...] = grid[...].astype(BF)


def combine(slots, info, parts, own, shape):
    smem = pl.BlockSpec(memory_space=pltpu.SMEM)
    return pl.pallas_call(
        combine_kernel,
        out_shape=jax.ShapeDtypeStruct(shape, BF),
        in_specs=[smem, smem, vmem(), hbm()],
        out_specs=vmem(),
        scratch_shapes=[
            pltpu.VMEM(shape, F32),
            pltpu.VMEM(own.shape, F32),
            pltpu.SemaphoreType.DMA,
        ],
        compiler_params=params(8),
        name="combine",
    )(slots, info, parts, keep(own))


def on_device(latents, prompt_rows, peg_weight, modulation_weight, qkv_weight, text_len, timestep):
    frames, tile_h, tile_w, width = latents.shape[1:]
    head_width = qkv_weight.shape[2]
    zl_at = lax.axis_index("zl")
    x_at = lax.axis_index("x")
    member = lax.axis_index("v") * 2 + zl_at

    shard = qkv_weight.reshape(qkv_weight.shape[0], 3 * head_width)
    weight = lax.all_gather(shard, ("item", "u", "v", "zl"), axis=0, tiled=True)
    padded = with_halo(latents, ((("u", "v", "zl"), 2), (("zh", "x"), 3)), 1)
    summed = latents.astype(F32)
    for row_tap in range(3):
        for col_tap in range(3):
            summed = summed + padded[
                :, :, row_tap : row_tap + tile_h, col_tap : col_tap + tile_w, :
            ].astype(F32) * peg_weight[row_tap, col_tap].astype(F32)
    peg = summed.astype(BF).reshape(frames * tile_h * tile_w, width)

    activation = jax.nn.silu(time_angles(timestep[0], modulation_weight.shape[0])).astype(BF)
    own_columns = jnp.dot(activation[None, :], modulation_weight, preferred_element_type=F32)
    rest = own_columns.reshape(3, 128)
    terms = []
    for _ in range(3):
        terms.append(lax.reduce_precision(rest, 8, 7))
        rest = rest - terms[-1]
    extra = jnp.concatenate(terms).astype(BF)
    extra = jnp.pad(extra, ((0, peg.shape[0] - 9), (0, 0)))
    peg = jnp.concatenate([peg, extra], axis=1)

    tokens = lax.all_gather(peg, "zh", axis=0, tiled=True)
    half = tokens.shape[0] // 2
    low, high = tokens[:half], tokens[half:]
    up = [(i, (i + 1) % 4) for i in range(4)]
    down = [(i, (i - 1) % 4) for i in range(4)]
    a0, b1 = lax.ppermute(low, "x", up), lax.ppermute(high, "x", down)
    a1, b0 = lax.ppermute(high, "x", up), lax.ppermute(low, "x", down)
    a0, b1 = lax.optimization_barrier((a0, b1))
    c0, c1 = lax.ppermute(a0, "x", up), lax.ppermute(b1, "x", down)
    pieces = (tokens, a0, a1, b0, b1, c0, c1)
    distance = (jnp.arange(4, dtype=jnp.int32) - x_at) % 4
    slots = jnp.where(distance == 0, 0, jnp.where(distance == 3, 1, distance + 1))

    lower = member * TEXT_PART
    start = jnp.minimum(lower, prompt_rows.shape[1] - TEXT_PART)
    text_rows = lax.dynamic_slice_in_dim(prompt_rows[0], start, TEXT_PART, axis=0)
    text_kv, q_copies, kv_copies = project(slots, pieces, text_rows, weight)
    group = ("v", "zl")
    qs = lax.all_to_all(q_copies, group, split_axis=0, concat_axis=0, tiled=True)
    kv = lax.all_to_all(kv_copies, "u", split_axis=0, concat_axis=0, tiled=True)
    info = jnp.stack([start, lower, text_len[0], member])
    count = qs.shape[1]
    part = jax.ShapeDtypeStruct((4, count + count // 128 * STAT_ROWS, 128), BF)
    parts = attend(peers_kernel, "peers", 3, part, info, qs, kv, text_kv)
    parts = lax.all_to_all(parts, group, split_axis=0, concat_axis=0, tiled=True)
    plain = jax.ShapeDtypeStruct((2, count, 128), F32)
    own = attend(own_kernel, "own", 1, plain, info, qs, kv, text_kv)
    shape = (frames, tile_h, 16 * tile_w, head_width)
    return combine(slots, info, parts, own, shape)[None]


def solution(mesh):
    fine = Mesh(mesh.devices.reshape(2, 4, 2, 2, 4, 4), ("item", "u", "v", "zl", "zh", "x"))
    row = ("u", "v", "zl")
    col = ("zh", "x")
    in_specs = (
        P("item", None, row, col, None),
        P("item", None, None),
        P(),
        P(None, col),
        P(("item",) + row, None, col),
        P("item"),
        P("item"),
    )
    out_specs = P("item", None, row, None, col)
    return jax.shard_map(
        on_device, mesh=fine, in_specs=in_specs, out_specs=out_specs, check_vma=False
    )
```

```python
import functools
import math

import jax
import jax.numpy as jnp
from jax import lax
from jax.experimental import pallas as pl
from jax.experimental.pallas import tpu as pltpu
from jax.sharding import Mesh, PartitionSpec as P

HD = 64
LOG2E = 1.4426950408889634
SCALE2 = 0.125 * LOG2E
BF = jnp.bfloat16
F32 = jnp.float32
TEXT_PART = 64
STAT_ROWS = 16


def vmem(*shape):
    return pl.BlockSpec(memory_space=pltpu.VMEM)


def hbm():
    return pl.BlockSpec(memory_space=pltpu.MemorySpace.HBM)


def keep(x):
    return pltpu.with_memory_space_constraint(x, pltpu.MemorySpace.HBM)


def params(mib):
    return pltpu.CompilerParams(vmem_limit_bytes=mib << 20)


def with_halo(block, sides, width):
    for axis, dim in sides:
        count = lax.axis_size(axis)
        forward = [(i, i + 1) for i in range(count - 1)]
        backward = [(target, source) for source, target in forward]
        low = lax.ppermute(
            lax.slice_in_dim(block, block.shape[dim] - width, None, axis=dim), axis, forward
        )
        high = lax.ppermute(lax.slice_in_dim(block, 0, width, axis=dim), axis, backward)
        block = jnp.concatenate([low, block, high], axis=dim)
    return block


def time_angles(step, count):
    half = count // 2
    freqs = jnp.exp(-math.log(10000.0) * jnp.arange(half, dtype=F32) / half)
    angle = step.astype(F32) * freqs
    return jnp.concatenate([jnp.cos(angle), jnp.sin(angle)])


def project_kernel(
    slots, x0, a0, a1, b0, b1, c0, c1, text, w_hbm,
    q_out, kv_out, text_out,
    held, mod, extra, normed, w_ref, kv, in_sems, w_sem, out_sems,
):
    rows = x0.shape[0]
    half = rows // 2
    width = text.shape[1]
    tile = rows // 4
    arrived = [(x0, 0)]
    for slot, (low, high) in enumerate(((a0, a1), (b0, b1), (c0, c1))):
        arrived += [(low, (slot + 1) * rows), (high, (slot + 1) * rows + half)]

    def tail(i):
        piece, at = arrived[i]
        size = piece.shape[0]
        return pltpu.make_async_copy(
            piece.at[:, pl.ds(width, 128)], extra.at[pl.ds(at, size), :], in_sems.at[0, i]
        )

    def body(i):
        piece, at = arrived[i]
        size = piece.shape[0]
        return pltpu.make_async_copy(
            piece.at[:, pl.ds(0, width)], held.at[pl.ds(at, size), :], in_sems.at[1, i]
        )

    count = len(arrived)
    for i in range(count):
        tail(i).start()
    for i in range(count):
        body(i).start()
    fetch = pltpu.make_async_copy(w_hbm, w_ref, w_sem)
    fetch.start()
    for i in range(count):
        tail(i).wait()
    for place in range(4):
        base = pl.multiple_of(slots[place] * rows, rows)
        terms = extra[pl.ds(base, rows), :].astype(F32)
        for far in range(4):
            for chunk in range(3):
                at = (far * 4 + place) * 3 + chunk
                kind, first = divmod(at * 128, width)
                row = far * tile + chunk
                mod[kind : kind + 1, first : first + 128] = (
                    terms[row : row + 1] + terms[row + 3 : row + 4] + terms[row + 6 : row + 7]
                )
    shift = mod[0:1, :]
    gain = 1.0 + mod[1:2, :]

    def norm(rows_in, at):
        values = rows_in.astype(F32)
        center = jnp.sum(values, axis=1, keepdims=True) * (1.0 / width)
        centered = values - center
        spread = jnp.sum(centered * centered, axis=1, keepdims=True) * (1.0 / width)
        result = centered * lax.rsqrt(spread + 1e-06) * gain + shift
        normed[at : at + rows_in.shape[0], :] = result.astype(BF)

    sends = []
    norm(text[...], 4 * rows)
    for part in range(2):
        first = 2 * rows * part
        for i in range(count):
            if first <= arrived[i][1] < first + 2 * rows:
                body(i).wait()
        for block in (2 * part, 2 * part + 1):
            norm(held[block * rows : (block + 1) * rows, :], block * rows)
        last = first + 2 * rows + (text.shape[0] if part else 0)
        if part == 0:
            fetch.wait()
        out = jnp.dot(normed[first:last, :], w_ref[...], preferred_element_type=F32).astype(BF)
        span = pl.ds(first, 2 * rows)
        q_out[span, :] = out[: 2 * rows, :128]
        kv[span, :] = out[: 2 * rows, 128:]
        sends.append(
            pltpu.make_async_copy(kv.at[span, :], kv_out.at[span, :], out_sems.at[part])
        )
        sends[-1].start()
        if part:
            text_out[...] = out[2 * rows :, 128:]
    for send in sends:
        send.wait()


def project(slots, pieces, text, weight):
    rows, lanes = pieces[0].shape
    width = text.shape[1]
    return pl.pallas_call(
        project_kernel,
        out_shape=[
            jax.ShapeDtypeStruct((4 * rows, 128), BF),
            pltpu.MemorySpace.HBM((4 * rows, 256), BF),
            jax.ShapeDtypeStruct((text.shape[0], 256), BF),
        ],
        in_specs=[pl.BlockSpec(memory_space=pltpu.SMEM)] + [hbm()] * 7 + [vmem(), hbm()],
        out_specs=[vmem(), hbm(), vmem()],
        scratch_shapes=[
            pltpu.VMEM((4 * rows, width), BF),
            pltpu.VMEM((2, width), F32),
            pltpu.VMEM((4 * rows, 128), BF),
            pltpu.VMEM((4 * rows + text.shape[0], width), BF),
            pltpu.VMEM(weight.shape, BF),
            pltpu.VMEM((4 * rows, 256), BF),
            pltpu.SemaphoreType.DMA((2, 7)),
            pltpu.SemaphoreType.DMA,
            pltpu.SemaphoreType.DMA((2,)),
        ],
        compiler_params=params(28),
        cost_estimate=pl.CostEstimate(
            flops=8 * rows * width * weight.shape[1],
            bytes_accessed=2 * (4 * rows * lanes + weight.size),
            transcendentals=4 * rows,
        ),
        name="project",
    )(slots, *map(keep, pieces), text, keep(weight))


def load_keys(kv, text_kv, keys, values):
    blocks, size = kv.shape[:2]
    for block in range(blocks):
        rows = pl.ds(block * size, size)
        keys[rows, :] = kv[block, :, :128]
        values[rows, :128] = kv[block, :, 128:]
    at = blocks * size
    pad = 128 - TEXT_PART
    keys[at : at + TEXT_PART, :] = text_kv[:, :128]
    keys[at + TEXT_PART :, :] = jnp.zeros((pad, 128), BF)
    values[at : at + TEXT_PART, :128] = text_kv[:, 128:]
    values[at + TEXT_PART :, :128] = jnp.zeros((pad, 128), BF)
    values[:, 128:] = jnp.ones((values.shape[0], 128), BF)


def softmax_block(info, q, keys, values):
    rows = q.shape[0]
    latent = keys.shape[0] - 128
    lane = lax.broadcasted_iota(jnp.int32, (rows, 128), 1)
    position = info[0] + lane
    valid = (position >= info[1]) & (position < info[2]) & (lane < TEXT_PART)
    q = q.astype(F32)
    outs, sums = [], []
    for head in range(2):
        own = jnp.where(lane // HD == head, q, 0.0).astype(BF)
        s = lax.dot_general(
            own, keys[...], (((1,), (1,)), ((), ())), preferred_element_type=F32
        )
        text = jnp.where(valid, s[:, latent:], -1e30)
        top = jnp.maximum(
            jnp.max(s[:, :latent], axis=1, keepdims=True), jnp.max(text, axis=1, keepdims=True)
        )
        top = top * SCALE2
        p = jnp.exp2(s[:, :latent] * SCALE2 - top).astype(BF)
        p_text = jnp.where(valid, jnp.exp2(text * SCALE2 - top), 0.0).astype(BF)
        p = jnp.concatenate([p, p_text], axis=1)
        acc = jnp.dot(p, values[...], preferred_element_type=F32)
        total = acc[:, 128:]
        outs.append(acc[:, :128] / total)
        sums.append(top + jnp.log(total) * LOG2E)
    return jnp.where(lane < HD, outs[0], outs[1]), jnp.where(lane < HD, sums[0], sums[1])


def peers_kernel(info, q1, q2, q3, kv, text_kv, o_ref, keys, values, held, sems):
    count = q1.shape[0]
    load_keys(kv, text_kv, keys, values)
    lane = lax.broadcasted_iota(jnp.int32, (128, 128), 1)

    def send(step):
        member = jnp.bitwise_xor(info[3], step)
        return pltpu.make_async_copy(held.at[step], o_ref.at[member], sems.at[step])

    for step, q_ref in enumerate((q1, q2, q3), 1):
        out, lse = softmax_block(info, q_ref[...], keys, values)
        held[step, :count, :] = out.astype(BF)
        for tile in range(count // 128):
            rest = lse[tile * 128 : (tile + 1) * 128]
            stats = jnp.zeros((128, 128), F32)
            for part in range(3):
                piece = rest.astype(BF).astype(F32)
                stats = jnp.where(lane % HD == part, piece, stats)
                rest = rest - piece
            across = jnp.transpose(stats)
            across = jnp.concatenate([across[:8], across[HD : HD + 8]], axis=0)
            at = count + tile * STAT_ROWS
            held[step, at : at + STAT_ROWS, :] = across.astype(BF)
        send(step).start()

    for step in range(1, 4):
        send(step).wait()


def own_kernel(info, q_ref, kv, text_kv, o_ref, keys, values, held, sems):
    load_keys(kv, text_kv, keys, values)
    out, lse = softmax_block(info, q_ref[...], keys, values)
    held[0] = out
    held[1] = lse
    copy = pltpu.make_async_copy(held, o_ref, sems.at[0])
    copy.start()
    copy.wait()


def attend(kernel, name, out_shape, info, qs, kv, text_kv):
    keys = kv.shape[0] * kv.shape[1] + 128
    blocks, count = len(qs), qs[0].shape[0]
    return pl.pallas_call(
        kernel,
        out_shape=pltpu.MemorySpace.HBM(out_shape.shape, out_shape.dtype),
        in_specs=[pl.BlockSpec(memory_space=pltpu.SMEM)] + [vmem()] * (blocks + 2),
        out_specs=hbm(),
        scratch_shapes=[
            pltpu.VMEM((keys, 128), BF),
            pltpu.VMEM((keys, 256), BF),
            pltpu.VMEM(out_shape.shape, out_shape.dtype),
            pltpu.SemaphoreType.DMA((4,)),
        ],
        compiler_params=params(24),
        cost_estimate=pl.CostEstimate(
            flops=4 * blocks * count * keys * 256,
            bytes_accessed=2 * (blocks * qs[0].size + kv.size),
            transcendentals=2 * blocks * count * keys,
        ),
        name=name,
    )(info, *qs, kv, text_kv)


def combine_kernel(slots, info, parts_ref, own_hbm, out, grid, own, sem):
    copy = pltpu.make_async_copy(own_hbm, own, sem)
    copy.start()
    o_ref, l_ref = own.at[0], own.at[1]
    members = parts_ref.shape[0]
    block = 128
    count = o_ref.shape[0]
    term = lax.broadcasted_iota(jnp.int32, (STAT_ROWS, 128), 0)
    head = lax.broadcasted_iota(jnp.int32, (STAT_ROWS, 128), 1) // HD
    spread = jnp.where((term // 8 == head) & (term % 8 < 3), 1.0, 0.0).astype(BF)
    frames, tile_h, cells = out.shape[:3]
    tile_w = cells // 16
    copy.wait()
    for place in range(4):
        slot = slots[place]
        rows = pl.ds(pl.multiple_of(slot * block, block), block)
        at = pl.ds(pl.multiple_of(count + slot * STAT_ROWS, STAT_ROWS), STAT_ROWS)
        lses = [l_ref[rows, :]]
        outs = [o_ref[rows, :]]
        for step in range(1, members):
            member = jnp.bitwise_xor(info[3], step)
            lses.append(
                lax.dot_general(
                    parts_ref[member, at, :],
                    spread,
                    (((0,), (0,)), ((), ())),
                    preferred_element_type=F32,
                )
            )
            outs.append(parts_ref[member, rows, :].astype(F32))
        top = functools.reduce(jnp.maximum, lses)
        shares = [jnp.exp2(lse - top) for lse in lses]
        weighted = sum(share * part for share, part in zip(shares, outs))
        merged = weighted / sum(shares)
        at = 0
        for far in range(4):
            for frame in range(frames):
                for row in range(tile_h):
                    first = (far * 4 + place) * tile_w
                    grid[frame, row, first : first + tile_w, :] = merged[at : at + tile_w]
                    at += tile_w
    out[...] = grid[...].astype(BF)


def combine(slots, info, parts, own, shape):
    smem = pl.BlockSpec(memory_space=pltpu.SMEM)
    return pl.pallas_call(
        combine_kernel,
        out_shape=jax.ShapeDtypeStruct(shape, BF),
        in_specs=[smem, smem, vmem(), hbm()],
        out_specs=vmem(),
        scratch_shapes=[
            pltpu.VMEM(shape, F32),
            pltpu.VMEM(own.shape, F32),
            pltpu.SemaphoreType.DMA,
        ],
        compiler_params=params(8),
        name="combine",
    )(slots, info, parts, keep(own))


def on_device(latents, prompt_rows, peg_weight, modulation_weight, qkv_weight, text_len, timestep):
    frames, tile_h, tile_w, width = latents.shape[1:]
    head_width = qkv_weight.shape[2]
    zl_at = lax.axis_index("zl")
    x_at = lax.axis_index("x")
    member = lax.axis_index("v") * 2 + zl_at

    row_axes = ("u", "v", "zl")
    padded = with_halo(latents, ((row_axes, 2), (("zh", "x"), 3)), 1)
    shard = qkv_weight.reshape(qkv_weight.shape[0], 3 * head_width)
    weight = lax.all_gather(shard, ("item",) + row_axes, axis=0, tiled=True)
    summed = latents.astype(F32)
    for row_tap in range(3):
        for col_tap in range(3):
            summed = summed + padded[
                :, :, row_tap : row_tap + tile_h, col_tap : col_tap + tile_w, :
            ].astype(F32) * peg_weight[row_tap, col_tap].astype(F32)
    peg = summed.astype(BF).reshape(frames * tile_h * tile_w, width)

    activation = jax.nn.silu(time_angles(timestep[0], modulation_weight.shape[0])).astype(BF)
    own_columns = jnp.dot(activation[None, :], modulation_weight, preferred_element_type=F32)
    rest = own_columns.reshape(3, 128)
    terms = []
    for _ in range(3):
        terms.append(lax.reduce_precision(rest, 8, 7))
        rest = rest - terms[-1]
    extra = jnp.concatenate(terms).astype(BF)
    extra = jnp.pad(extra, ((0, peg.shape[0] - 9), (0, 0)))
    peg = jnp.concatenate([peg, extra], axis=1)

    tokens = lax.all_gather(peg, "zh", axis=0, tiled=True)
    half = tokens.shape[0] // 2
    low, high = tokens[:half], tokens[half:]
    up = [(i, (i + 1) % 4) for i in range(4)]
    down = [(i, (i - 1) % 4) for i in range(4)]
    a0, b1 = lax.ppermute(low, "x", up), lax.ppermute(high, "x", down)
    a1, b0 = lax.ppermute(high, "x", up), lax.ppermute(low, "x", down)
    a0, b1 = lax.optimization_barrier((a0, b1))
    c0, c1 = lax.ppermute(a0, "x", up), lax.ppermute(b1, "x", down)
    pieces = (tokens, a0, a1, b0, b1, c0, c1)
    distance = (jnp.arange(4, dtype=jnp.int32) - x_at) % 4
    slots = jnp.where(distance == 0, 0, jnp.where(distance == 3, 1, distance + 1))

    lower = member * TEXT_PART
    start = jnp.minimum(lower, prompt_rows.shape[1] - TEXT_PART)
    text_rows = lax.dynamic_slice_in_dim(prompt_rows[0], start, TEXT_PART, axis=0)
    queries, kv, text_kv = project(slots, pieces, text_rows, weight)
    group = ("v", "zl")
    swaps = (
        ("zl", [(0, 1), (1, 0)]),
        ("v", [(0, 1), (1, 0)]),
        (group, [(0, 3), (3, 0), (1, 2), (2, 1)]),
    )
    qs = [lax.ppermute(queries, axis, swap) for axis, swap in swaps]
    kv = lax.all_gather(kv, "u", axis=0)
    info = jnp.stack([start, lower, text_len[0], member])
    count = queries.shape[0]
    part = jax.ShapeDtypeStruct((4, count + count // 128 * STAT_ROWS, 128), BF)
    parts = attend(peers_kernel, "peers", part, info, qs, kv, text_kv)
    parts = lax.all_to_all(parts, group, split_axis=0, concat_axis=0, tiled=True)
    plain = jax.ShapeDtypeStruct((2, count, 128), F32)
    own = attend(own_kernel, "own", plain, info, [queries], kv, text_kv)
    shape = (frames, tile_h, 16 * tile_w, head_width)
    return combine(slots, info, parts, own, shape)[None]


def solution(mesh):
    fine = Mesh(mesh.devices.reshape(2, 4, 2, 2, 4, 4), ("item", "u", "v", "zl", "zh", "x"))
    row = ("u", "v", "zl")
    col = ("zh", "x")
    in_specs = (
        P("item", None, row, col, None),
        P("item", None, None),
        P(),
        P(None, col),
        P(("item",) + row, None, col),
        P("item"),
        P("item"),
    )
    out_specs = P("item", None, row, None, col)
    return jax.shard_map(
        on_device, mesh=fine, in_specs=in_specs, out_specs=out_specs, check_vma=False
    )
```

```python
import functools
import math

import jax
import jax.numpy as jnp
from jax import lax
from jax.experimental import pallas as pl
from jax.experimental.pallas import tpu as pltpu
from jax.sharding import Mesh, PartitionSpec as P

HD = 64
LOG2E = 1.4426950408889634
SCALE2 = 0.125 * LOG2E
BF = jnp.bfloat16
F32 = jnp.float32
TEXT_PART = 64
STAT_ROWS = 16


def vmem(*shape):
    return pl.BlockSpec(memory_space=pltpu.VMEM)


def hbm():
    return pl.BlockSpec(memory_space=pltpu.MemorySpace.HBM)


def keep(x):
    return pltpu.with_memory_space_constraint(x, pltpu.MemorySpace.HBM)


def params(mib):
    return pltpu.CompilerParams(vmem_limit_bytes=mib << 20)


def with_halo(block, sides, width):
    for axis, dim in sides:
        count = lax.axis_size(axis)
        forward = [(i, i + 1) for i in range(count - 1)]
        backward = [(target, source) for source, target in forward]
        low = lax.ppermute(
            lax.slice_in_dim(block, block.shape[dim] - width, None, axis=dim), axis, forward
        )
        high = lax.ppermute(lax.slice_in_dim(block, 0, width, axis=dim), axis, backward)
        block = jnp.concatenate([low, block, high], axis=dim)
    return block


def time_angles(step, count):
    half = count // 2
    freqs = jnp.exp(-math.log(10000.0) * jnp.arange(half, dtype=F32) / half)
    angle = step.astype(F32) * freqs
    return jnp.concatenate([jnp.cos(angle), jnp.sin(angle)])


def project_kernel(
    slots, x0, a0, a1, b0, b1, c0, c1, text, w_hbm,
    q_out, kv_out, text_out,
    held, mod, extra, normed, w_ref, kv, in_sems, w_sem, out_sems,
):
    rows = x0.shape[0]
    half = rows // 2
    width = text.shape[1]
    tile = rows // 4
    arrived = [(x0, 0)]
    for slot, (low, high) in enumerate(((a0, a1), (b0, b1), (c0, c1))):
        arrived += [(low, (slot + 1) * rows), (high, (slot + 1) * rows + half)]

    def tail(i):
        piece, at = arrived[i]
        size = piece.shape[0]
        return pltpu.make_async_copy(
            piece.at[:, pl.ds(width, 128)], extra.at[pl.ds(at, size), :], in_sems.at[0, i]
        )

    def body(i):
        piece, at = arrived[i]
        size = piece.shape[0]
        return pltpu.make_async_copy(
            piece.at[:, pl.ds(0, width)], held.at[pl.ds(at, size), :], in_sems.at[1, i]
        )

    count = len(arrived)
    for i in range(count):
        tail(i).start()
    for i in range(count):
        body(i).start()
    fetch = pltpu.make_async_copy(w_hbm, w_ref, w_sem)
    fetch.start()
    for i in range(count):
        tail(i).wait()
    for place in range(4):
        base = pl.multiple_of(slots[place] * rows, rows)
        terms = extra[pl.ds(base, rows), :].astype(F32)
        for far in range(4):
            for chunk in range(3):
                at = (far * 4 + place) * 3 + chunk
                kind, first = divmod(at * 128, width)
                row = far * tile + chunk
                mod[kind : kind + 1, first : first + 128] = (
                    terms[row : row + 1] + terms[row + 3 : row + 4] + terms[row + 6 : row + 7]
                )
    shift = mod[0:1, :]
    gain = 1.0 + mod[1:2, :]

    def norm(rows_in, at):
        values = rows_in.astype(F32)
        center = jnp.sum(values, axis=1, keepdims=True) * (1.0 / width)
        centered = values - center
        spread = jnp.sum(centered * centered, axis=1, keepdims=True) * (1.0 / width)
        result = centered * lax.rsqrt(spread + 1e-06) * gain + shift
        normed[at : at + rows_in.shape[0], :] = result.astype(BF)

    sends = []
    norm(text[...], 4 * rows)
    for part in range(2):
        first = 2 * rows * part
        for i in range(count):
            if first <= arrived[i][1] < first + 2 * rows:
                body(i).wait()
        for block in (2 * part, 2 * part + 1):
            norm(held[block * rows : (block + 1) * rows, :], block * rows)
        last = first + 2 * rows + (text.shape[0] if part else 0)
        if part == 0:
            fetch.wait()
        out = jnp.dot(normed[first:last, :], w_ref[...], preferred_element_type=F32).astype(BF)
        span = pl.ds(first, 2 * rows)
        q_out[span, :] = out[: 2 * rows, :128]
        kv[span, :] = out[: 2 * rows, 128:]
        sends.append(
            pltpu.make_async_copy(kv.at[span, :], kv_out.at[span, :], out_sems.at[part])
        )
        sends[-1].start()
        if part:
            text_out[...] = out[2 * rows :, 128:]
    for send in sends:
        send.wait()


def project(slots, pieces, text, weight):
    rows, lanes = pieces[0].shape
    width = text.shape[1]
    return pl.pallas_call(
        project_kernel,
        out_shape=[
            jax.ShapeDtypeStruct((4 * rows, 128), BF),
            pltpu.MemorySpace.HBM((4 * rows, 256), BF),
            jax.ShapeDtypeStruct((text.shape[0], 256), BF),
        ],
        in_specs=[pl.BlockSpec(memory_space=pltpu.SMEM)] + [hbm()] * 7 + [vmem(), hbm()],
        out_specs=[vmem(), hbm(), vmem()],
        scratch_shapes=[
            pltpu.VMEM((4 * rows, width), BF),
            pltpu.VMEM((2, width), F32),
            pltpu.VMEM((4 * rows, 128), BF),
            pltpu.VMEM((4 * rows + text.shape[0], width), BF),
            pltpu.VMEM(weight.shape, BF),
            pltpu.VMEM((4 * rows, 256), BF),
            pltpu.SemaphoreType.DMA((2, 7)),
            pltpu.SemaphoreType.DMA,
            pltpu.SemaphoreType.DMA((2,)),
        ],
        compiler_params=params(28),
        cost_estimate=pl.CostEstimate(
            flops=8 * rows * width * weight.shape[1],
            bytes_accessed=2 * (4 * rows * lanes + weight.size),
            transcendentals=4 * rows,
        ),
        name="project",
    )(slots, *map(keep, pieces), text, keep(weight))


def load_keys(blocks, text_kv, keys, values):
    at = 0
    for block in blocks:
        size = block.shape[0]
        keys[at : at + size, :] = block[:, :128]
        values[at : at + size, :128] = block[:, 128:]
        at += size
    if text_kv is not None:
        pad = 128 - TEXT_PART
        keys[at : at + TEXT_PART, :] = text_kv[:, :128]
        keys[at + TEXT_PART :, :] = jnp.zeros((pad, 128), BF)
        values[at : at + TEXT_PART, :128] = text_kv[:, 128:]
        values[at + TEXT_PART :, :128] = jnp.zeros((pad, 128), BF)
    values[:, 128:] = jnp.ones((values.shape[0], 128), BF)


def softmax_block(info, q, keys, values, has_text):
    rows = q.shape[0]
    latent = keys.shape[0] - (128 if has_text else 0)
    lane = lax.broadcasted_iota(jnp.int32, (rows, 128), 1)
    position = info[0] + lane
    valid = (position >= info[1]) & (position < info[2]) & (lane < TEXT_PART)
    q = q.astype(F32)
    outs, sums = [], []
    for head in range(2):
        own = jnp.where(lane // HD == head, q, 0.0).astype(BF)
        s = lax.dot_general(
            own, keys[...], (((1,), (1,)), ((), ())), preferred_element_type=F32
        )
        top = jnp.max(s[:, :latent], axis=1, keepdims=True)
        if has_text:
            text = jnp.where(valid, s[:, latent:], -1e30)
            top = jnp.maximum(top, jnp.max(text, axis=1, keepdims=True))
        top = top * SCALE2
        p = jnp.exp2(s[:, :latent] * SCALE2 - top).astype(BF)
        if has_text:
            p_text = jnp.where(valid, jnp.exp2(text * SCALE2 - top), 0.0).astype(BF)
            p = jnp.concatenate([p, p_text], axis=1)
        acc = jnp.dot(p, values[...], preferred_element_type=F32)
        total = acc[:, 128:]
        outs.append(acc[:, :128] / total)
        sums.append(top + jnp.log(total) * LOG2E)
    return jnp.where(lane < HD, outs[0], outs[1]), jnp.where(lane < HD, sums[0], sums[1])


def first_kernel(info, q1, q2, q3, kv0, kv1, kv2, text_kv, o_ref, keys, values, held, sems):
    load_keys((kv0, kv1, kv2), text_kv, keys, values)
    sends = []
    for i, q_ref in enumerate((q1, q2, q3)):
        held[i, 0], held[i, 1] = softmax_block(info, q_ref[...], keys, values, True)
        sends.append(pltpu.make_async_copy(held.at[i], o_ref.at[i], sems.at[i]))
        sends[-1].start()
    for send in sends:
        send.wait()


def rest_kernel(
    info, q1, q2, q3, kv3, kv4, before_hbm, o_ref, keys, values, held, before, sems, in_sems
):
    fetches = [
        pltpu.make_async_copy(before_hbm.at[i], before.at[i], in_sems.at[i]) for i in range(3)
    ]
    for fetch in fetches:
        fetch.start()
    count = q1.shape[0]
    load_keys((kv3, kv4), None, keys, values)
    lane = lax.broadcasted_iota(jnp.int32, (128, 128), 1)
    sends = []
    for i, q_ref in enumerate((q1, q2, q3)):
        out, lse = softmax_block(info, q_ref[...], keys, values, False)
        fetches[i].wait()
        earlier = before[i, 1]
        top = jnp.maximum(lse, earlier)
        new, old = jnp.exp2(lse - top), jnp.exp2(earlier - top)
        total = new + old
        held[i, :count, :] = ((new * out + old * before[i, 0]) / total).astype(BF)
        lse = top + jnp.log(total) * LOG2E
        for tile in range(count // 128):
            rest = lse[tile * 128 : (tile + 1) * 128]
            stats = jnp.zeros((128, 128), F32)
            for part in range(3):
                piece = rest.astype(BF).astype(F32)
                stats = jnp.where(lane % HD == part, piece, stats)
                rest = rest - piece
            across = jnp.transpose(stats)
            across = jnp.concatenate([across[:8], across[HD : HD + 8]], axis=0)
            at = count + tile * STAT_ROWS
            held[i, at : at + STAT_ROWS, :] = across.astype(BF)
        member = jnp.bitwise_xor(info[3], i + 1)
        sends.append(pltpu.make_async_copy(held.at[i], o_ref.at[member], sems.at[i]))
        sends[-1].start()
    for send in sends:
        send.wait()


def own_kernel(info, q_ref, kv0, kv1, kv2, kv3, kv4, text_kv, o_ref, keys, values, held, sems):
    load_keys((kv0, kv1, kv2, kv3, kv4), text_kv, keys, values)
    held[0], held[1] = softmax_block(info, q_ref[...], keys, values, True)
    copy = pltpu.make_async_copy(held, o_ref, sems.at[0])
    copy.start()
    copy.wait()


def attend(kernel, name, out_shape, held, info, qs, blocks, text_kv=None, before=None):
    keys = sum(block.shape[0] for block in blocks) + (0 if text_kv is None else 128)
    count = qs[0].shape[0]
    operands = [*qs, *blocks] + ([] if text_kv is None else [text_kv])
    specs = [pl.BlockSpec(memory_space=pltpu.SMEM)] + [vmem()] * len(operands)
    scratch = [
        pltpu.VMEM((keys, 128), BF),
        pltpu.VMEM((keys, 256), BF),
        pltpu.VMEM(held, out_shape.dtype),
    ]
    sems = [pltpu.SemaphoreType.DMA((3,))]
    if before is not None:
        operands.append(keep(before))
        specs.append(hbm())
        scratch.append(pltpu.VMEM(before.shape, before.dtype))
        sems = sems * 2
    return pl.pallas_call(
        kernel,
        out_shape=pltpu.MemorySpace.HBM(out_shape.shape, out_shape.dtype),
        in_specs=specs,
        out_specs=hbm(),
        scratch_shapes=scratch + sems,
        compiler_params=params(24),
        cost_estimate=pl.CostEstimate(
            flops=4 * len(qs) * count * keys * 256,
            bytes_accessed=512 * (len(qs) * count + keys),
            transcendentals=2 * len(qs) * count * keys,
        ),
        name=name,
    )(info, *operands)


def combine_kernel(slots, info, parts_ref, own_hbm, out, grid, own, sem):
    copy = pltpu.make_async_copy(own_hbm, own, sem)
    copy.start()
    o_ref, l_ref = own.at[0], own.at[1]
    members = parts_ref.shape[0]
    block = 128
    count = o_ref.shape[0]
    term = lax.broadcasted_iota(jnp.int32, (STAT_ROWS, 128), 0)
    head = lax.broadcasted_iota(jnp.int32, (STAT_ROWS, 128), 1) // HD
    spread = jnp.where((term // 8 == head) & (term % 8 < 3), 1.0, 0.0).astype(BF)
    frames, tile_h, cells = out.shape[:3]
    tile_w = cells // 16
    copy.wait()
    for place in range(4):
        slot = slots[place]
        rows = pl.ds(pl.multiple_of(slot * block, block), block)
        at = pl.ds(pl.multiple_of(count + slot * STAT_ROWS, STAT_ROWS), STAT_ROWS)
        lses = [l_ref[rows, :]]
        outs = [o_ref[rows, :]]
        for step in range(1, members):
            member = jnp.bitwise_xor(info[3], step)
            lses.append(
                lax.dot_general(
                    parts_ref[member, at, :],
                    spread,
                    (((0,), (0,)), ((), ())),
                    preferred_element_type=F32,
                )
            )
            outs.append(parts_ref[member, rows, :].astype(F32))
        top = functools.reduce(jnp.maximum, lses)
        shares = [jnp.exp2(lse - top) for lse in lses]
        weighted = sum(share * part for share, part in zip(shares, outs))
        merged = weighted / sum(shares)
        at = 0
        for far in range(4):
            for frame in range(frames):
                for row in range(tile_h):
                    first = (far * 4 + place) * tile_w
                    grid[frame, row, first : first + tile_w, :] = merged[at : at + tile_w]
                    at += tile_w
    out[...] = grid[...].astype(BF)


def combine(slots, info, parts, own, shape):
    smem = pl.BlockSpec(memory_space=pltpu.SMEM)
    return pl.pallas_call(
        combine_kernel,
        out_shape=jax.ShapeDtypeStruct(shape, BF),
        in_specs=[smem, smem, vmem(), hbm()],
        out_specs=vmem(),
        scratch_shapes=[
            pltpu.VMEM(shape, F32),
            pltpu.VMEM(own.shape, F32),
            pltpu.SemaphoreType.DMA,
        ],
        compiler_params=params(8),
        name="combine",
    )(slots, info, parts, keep(own))


def on_device(latents, prompt_rows, peg_weight, modulation_weight, qkv_weight, text_len, timestep):
    frames, tile_h, tile_w, width = latents.shape[1:]
    head_width = qkv_weight.shape[2]
    zl_at = lax.axis_index("zl")
    x_at = lax.axis_index("x")
    member = lax.axis_index("v") * 2 + zl_at

    row_axes = ("u", "v", "zl")
    padded = with_halo(latents, ((row_axes, 2),), 1)
    padded, peg_weight, modulation_weight = lax.optimization_barrier(
        (padded, peg_weight, modulation_weight)
    )
    padded = with_halo(padded, ((("zh", "x"), 3),), 1)
    shard = qkv_weight.reshape(qkv_weight.shape[0], 3 * head_width)
    weight = lax.all_gather(shard, ("item",) + row_axes, axis=0, tiled=True)
    summed = latents.astype(F32)
    for row_tap in range(3):
        for col_tap in range(3):
            summed = summed + padded[
                :, :, row_tap : row_tap + tile_h, col_tap : col_tap + tile_w, :
            ].astype(F32) * peg_weight[row_tap, col_tap].astype(F32)
    peg = summed.astype(BF).reshape(frames * tile_h * tile_w, width)

    activation = jax.nn.silu(time_angles(timestep[0], modulation_weight.shape[0])).astype(BF)
    own_columns = jnp.dot(activation[None, :], modulation_weight, preferred_element_type=F32)
    rest = own_columns.reshape(3, 128)
    terms = []
    for _ in range(3):
        terms.append(lax.reduce_precision(rest, 8, 7))
        rest = rest - terms[-1]
    extra = jnp.concatenate(terms).astype(BF)
    extra = jnp.pad(extra, ((0, peg.shape[0] - 9), (0, 0)))
    peg = jnp.concatenate([peg, extra], axis=1)

    tokens = lax.all_gather(peg, "zh", axis=0, tiled=True)
    half = tokens.shape[0] // 2
    low, high = tokens[:half], tokens[half:]
    up = [(i, (i + 1) % 4) for i in range(4)]
    down = [(i, (i - 1) % 4) for i in range(4)]
    a0, b1 = lax.ppermute(low, "x", up), lax.ppermute(high, "x", down)
    a1, b0 = lax.ppermute(high, "x", up), lax.ppermute(low, "x", down)
    a0, b1 = lax.optimization_barrier((a0, b1))
    c0, c1 = lax.ppermute(a0, "x", up), lax.ppermute(b1, "x", down)
    pieces = (tokens, a0, a1, b0, b1, c0, c1)
    distance = (jnp.arange(4, dtype=jnp.int32) - x_at) % 4
    slots = jnp.where(distance == 0, 0, jnp.where(distance == 3, 1, distance + 1))

    lower = member * TEXT_PART
    start = jnp.minimum(lower, prompt_rows.shape[1] - TEXT_PART)
    text_rows = lax.dynamic_slice_in_dim(prompt_rows[0], start, TEXT_PART, axis=0)
    queries, kv, text_kv = project(slots, pieces, text_rows, weight)
    group = ("v", "zl")
    swaps = (
        ("zl", [(0, 1), (1, 0)]),
        ("v", [(0, 1), (1, 0)]),
        (group, [(0, 3), (3, 0), (1, 2), (2, 1)]),
    )
    qs = [lax.ppermute(queries, axis, swap) for axis, swap in swaps]
    near = [lax.ppermute(kv, "u", up), lax.ppermute(kv, "u", down)]
    near = lax.optimization_barrier(near)
    count = kv.shape[0]
    far = [
        lax.ppermute(near[0][: count // 2], "u", up),
        lax.ppermute(near[1][count // 2 :], "u", down),
    ]
    info = jnp.stack([start, lower, text_len[0], member])
    shape = (3, 2, count, 128)
    first = jax.ShapeDtypeStruct(shape, F32)
    first = attend(first_kernel, "first", first, shape, info, qs, [kv, *near], text_kv)
    shape = (4, count + count // 128 * STAT_ROWS, 128)
    parts = jax.ShapeDtypeStruct(shape, BF)
    parts = attend(rest_kernel, "rest", parts, (3,) + shape[1:], info, qs, far, None, first)
    parts = lax.all_to_all(parts, group, split_axis=0, concat_axis=0, tiled=True)
    shape = (2, count, 128)
    own = jax.ShapeDtypeStruct(shape, F32)
    own = attend(own_kernel, "own", own, shape, info, [queries], [kv, *near, *far], text_kv)
    shape = (frames, tile_h, 16 * tile_w, head_width)
    return combine(slots, info, parts, own, shape)[None]


def solution(mesh):
    fine = Mesh(mesh.devices.reshape(2, 4, 2, 2, 4, 4), ("item", "u", "v", "zl", "zh", "x"))
    row = ("u", "v", "zl")
    col = ("zh", "x")
    in_specs = (
        P("item", None, row, col, None),
        P("item", None, None),
        P(),
        P(None, col),
        P(("item",) + row, None, col),
        P("item"),
        P("item"),
    )
    out_specs = P("item", None, row, None, col)
    return jax.shard_map(
        on_device, mesh=fine, in_specs=in_specs, out_specs=out_specs, check_vma=False
    )
```

```python
import functools
import math

import jax
import jax.numpy as jnp
from jax import lax
from jax.experimental import pallas as pl
from jax.experimental.pallas import tpu as pltpu
from jax.sharding import Mesh, PartitionSpec as P

HD = 64
LOG2E = 1.4426950408889634
SCALE2 = 0.125 * LOG2E
BF = jnp.bfloat16
F32 = jnp.float32
TEXT_PART = 64
STAT_ROWS = 16


def vmem(*shape):
    return pl.BlockSpec(memory_space=pltpu.VMEM)


def hbm():
    return pl.BlockSpec(memory_space=pltpu.MemorySpace.HBM)


def keep(x):
    return pltpu.with_memory_space_constraint(x, pltpu.MemorySpace.HBM)


def params(mib):
    return pltpu.CompilerParams(vmem_limit_bytes=mib << 20)


def with_halo(block, sides, width):
    for axis, dim in sides:
        count = lax.axis_size(axis)
        forward = [(i, i + 1) for i in range(count - 1)]
        backward = [(target, source) for source, target in forward]
        low = lax.ppermute(
            lax.slice_in_dim(block, block.shape[dim] - width, None, axis=dim), axis, forward
        )
        high = lax.ppermute(lax.slice_in_dim(block, 0, width, axis=dim), axis, backward)
        block = jnp.concatenate([low, block, high], axis=dim)
    return block


def time_angles(step, count):
    half = count // 2
    freqs = jnp.exp(-math.log(10000.0) * jnp.arange(half, dtype=F32) / half)
    angle = step.astype(F32) * freqs
    return jnp.concatenate([jnp.cos(angle), jnp.sin(angle)])


def project_kernel(
    slots, x0, x1, a0, a1, b0, b1, c0, c1, text, w_hbm,
    q_out, kv_out, text_out,
    held, mod, extra, normed, w_ref, q, kv, in_sems, w_sem, out_sems,
):
    half = x0.shape[0]
    rows = 2 * half
    width = text.shape[1]
    tile = rows // 4
    arrived = []
    for slot, (low, high) in enumerate(((x0, x1), (a0, a1), (b0, b1), (c0, c1))):
        arrived += [(low, slot * rows), (high, slot * rows + half)]

    def tail(i):
        piece, at = arrived[i]
        size = piece.shape[0]
        return pltpu.make_async_copy(
            piece.at[:, pl.ds(width, 128)], extra.at[pl.ds(at, size), :], in_sems.at[0, i]
        )

    def body(i):
        piece, at = arrived[i]
        size = piece.shape[0]
        return pltpu.make_async_copy(
            piece.at[:, pl.ds(0, width)], held.at[pl.ds(at, size), :], in_sems.at[1, i]
        )

    count = len(arrived)
    for i in range(count):
        tail(i).start()
    for i in range(count):
        body(i).start()
    fetch = pltpu.make_async_copy(w_hbm, w_ref, w_sem)
    fetch.start()
    for i in range(count):
        tail(i).wait()
    for place in range(4):
        base = pl.multiple_of(slots[place] * rows, rows)
        terms = extra[pl.ds(base, rows), :].astype(F32)
        for far in range(4):
            for chunk in range(3):
                at = (far * 4 + place) * 3 + chunk
                kind, first = divmod(at * 128, width)
                row = far * tile + chunk
                mod[kind : kind + 1, first : first + 128] = (
                    terms[row : row + 1] + terms[row + 3 : row + 4] + terms[row + 6 : row + 7]
                )
    shift = mod[0:1, :]
    gain = 1.0 + mod[1:2, :]

    def norm(rows_in, at):
        values = rows_in.astype(F32)
        center = jnp.sum(values, axis=1, keepdims=True) * (1.0 / width)
        centered = values - center
        spread = jnp.sum(centered * centered, axis=1, keepdims=True) * (1.0 / width)
        result = centered * lax.rsqrt(spread + 1e-06) * gain + shift
        normed[at : at + rows_in.shape[0], :] = result.astype(BF)

    sends = []
    norm(text[...], 4 * rows)
    for part in range(2):
        first = 2 * rows * part
        for i in range(count):
            if first <= arrived[i][1] < first + 2 * rows:
                body(i).wait()
        for block in (2 * part, 2 * part + 1):
            norm(held[block * rows : (block + 1) * rows, :], block * rows)
        last = first + 2 * rows + (text.shape[0] if part else 0)
        if part == 0:
            fetch.wait()
        out = jnp.dot(normed[first:last, :], w_ref[...], preferred_element_type=F32).astype(BF)
        span = pl.ds(first, 2 * rows)
        q[span, :] = out[: 2 * rows, :128]
        kv[span, :] = out[: 2 * rows, 128:]
        new = [pltpu.make_async_copy(kv.at[span, :], kv_out.at[span, :], out_sems.at[part, 4])]
        for i in range(4):
            new.append(
                pltpu.make_async_copy(q.at[span, :], q_out.at[i, span, :], out_sems.at[part, i])
            )
        for send in new:
            send.start()
        sends += new
        if part:
            text_out[...] = out[2 * rows :, 128:]
    for send in sends:
        send.wait()


def project(slots, pieces, text, weight):
    half, lanes = pieces[0].shape
    rows = 2 * half
    width = text.shape[1]
    return pl.pallas_call(
        project_kernel,
        out_shape=[
            pltpu.MemorySpace.HBM((4, 4 * rows, 128), BF),
            pltpu.MemorySpace.HBM((4 * rows, 256), BF),
            jax.ShapeDtypeStruct((text.shape[0], 256), BF),
        ],
        in_specs=[pl.BlockSpec(memory_space=pltpu.SMEM)] + [hbm()] * 8 + [vmem(), hbm()],
        out_specs=[hbm(), hbm(), vmem()],
        scratch_shapes=[
            pltpu.VMEM((4 * rows, width), BF),
            pltpu.VMEM((2, width), F32),
            pltpu.VMEM((4 * rows, 128), BF),
            pltpu.VMEM((4 * rows + text.shape[0], width), BF),
            pltpu.VMEM(weight.shape, BF),
            pltpu.VMEM((4 * rows, 128), BF),
            pltpu.VMEM((4 * rows, 256), BF),
            pltpu.SemaphoreType.DMA((2, 8)),
            pltpu.SemaphoreType.DMA,
            pltpu.SemaphoreType.DMA((2, 5)),
        ],
        compiler_params=params(28),
        cost_estimate=pl.CostEstimate(
            flops=8 * rows * width * weight.shape[1],
            bytes_accessed=2 * (4 * rows * lanes + weight.size),
            transcendentals=4 * rows,
        ),
        name="project",
    )(slots, *map(keep, pieces), text, keep(weight))


def load_keys(blocks, text_kv, keys, values):
    at = 0
    for block in blocks:
        size = block.shape[0]
        keys[at : at + size, :] = block[:, :128]
        values[at : at + size, :128] = block[:, 128:]
        at += size
    if text_kv is not None:
        pad = 128 - TEXT_PART
        keys[at : at + TEXT_PART, :] = text_kv[:, :128]
        keys[at + TEXT_PART :, :] = jnp.zeros((pad, 128), BF)
        values[at : at + TEXT_PART, :128] = text_kv[:, 128:]
        values[at + TEXT_PART :, :128] = jnp.zeros((pad, 128), BF)
    values[:, 128:] = jnp.ones((values.shape[0], 128), BF)


def softmax_block(info, q, keys, values, has_text):
    rows = q.shape[0]
    latent = keys.shape[0] - (128 if has_text else 0)
    lane = lax.broadcasted_iota(jnp.int32, (rows, 128), 1)
    position = info[0] + lane
    valid = (position >= info[1]) & (position < info[2]) & (lane < TEXT_PART)
    q = q.astype(F32)
    accs, tops = [], []
    for head in range(2):
        own = jnp.where(lane // HD == head, q, 0.0).astype(BF)
        s = lax.dot_general(
            own, keys[...], (((1,), (1,)), ((), ())), preferred_element_type=F32
        )
        top = jnp.max(s[:, :latent], axis=1, keepdims=True)
        if has_text:
            text = jnp.where(valid, s[:, latent:], -1e30)
            top = jnp.maximum(top, jnp.max(text, axis=1, keepdims=True))
        top = top * SCALE2
        p = jnp.exp2(s[:, :latent] * SCALE2 - top).astype(BF)
        if has_text:
            p_text = jnp.where(valid, jnp.exp2(text * SCALE2 - top), 0.0).astype(BF)
            p = jnp.concatenate([p, p_text], axis=1)
        accs.append(jnp.dot(p, values[...], preferred_element_type=F32))
        tops.append(top)
    total = jnp.where(lane < HD, accs[0][:, 128:], accs[1][:, 128:])
    weighted = jnp.where(lane < HD, accs[0][:, :128], accs[1][:, :128])
    return weighted / total, jnp.where(lane < HD, tops[0], tops[1]) + jnp.log(total) * LOG2E


def first_kernel(info, q_ref, kv0, kv1, kv2, text_kv, o_ref, keys, values, held, sems):
    load_keys((kv0, kv1, kv2), text_kv, keys, values)
    sends = []
    for i in range(3):
        q = q_ref[jnp.bitwise_xor(info[3], i + 1)]
        held[i, 0], held[i, 1] = softmax_block(info, q, keys, values, True)
        sends.append(pltpu.make_async_copy(held.at[i], o_ref.at[i], sems.at[i]))
        sends[-1].start()
    for send in sends:
        send.wait()


def rest_kernel(
    info, q_ref, kv3, kv4, before_hbm, o_ref, keys, values, held, before, sems, in_sems
):
    fetches = [
        pltpu.make_async_copy(before_hbm.at[i], before.at[i], in_sems.at[i]) for i in range(3)
    ]
    for fetch in fetches:
        fetch.start()
    count = q_ref.shape[1]
    load_keys((kv3, kv4), None, keys, values)
    term = lax.broadcasted_iota(jnp.int32, (STAT_ROWS, 128), 0)
    lane = lax.broadcasted_iota(jnp.int32, (STAT_ROWS, 128), 1)
    sends = []
    for i in range(3):
        member = jnp.bitwise_xor(info[3], i + 1)
        out, lse = softmax_block(info, q_ref[member], keys, values, False)
        fetches[i].wait()
        earlier = before[i, 1]
        top = jnp.maximum(lse, earlier)
        new, old = jnp.exp2(lse - top), jnp.exp2(earlier - top)
        total = new + old
        held[i, :count, :] = ((new * out + old * before[i, 0]) / total).astype(BF)
        lse = top + jnp.log(total) * LOG2E
        across = jnp.zeros((STAT_ROWS, count), F32)
        for part in range(3):
            piece = lse.astype(BF)
            lse = lse - piece.astype(F32)
            pick = jnp.where((term % 8 == part) & (lane == term // 8 * HD), 1.0, 0.0).astype(BF)
            across = across + lax.dot_general(
                pick, piece, (((1,), (1,)), ((), ())), preferred_element_type=F32
            )
        for tile in range(count // 128):
            at = count + tile * STAT_ROWS
            held[i, at : at + STAT_ROWS, :] = across[:, tile * 128 : (tile + 1) * 128].astype(BF)
        sends.append(pltpu.make_async_copy(held.at[i], o_ref.at[member], sems.at[i]))
        sends[-1].start()
    for send in sends:
        send.wait()


def own_kernel(info, q_ref, kv0, kv1, kv2, kv3, kv4, text_kv, o_ref, keys, values, held, sems):
    load_keys((kv0, kv1, kv2, kv3, kv4), text_kv, keys, values)
    held[0], held[1] = softmax_block(info, q_ref[info[3]], keys, values, True)
    copy = pltpu.make_async_copy(held, o_ref, sems.at[0])
    copy.start()
    copy.wait()


def attend(kernel, name, peers, out_shape, held, info, qs, blocks, text_kv=None, before=None):
    keys = sum(block.shape[0] for block in blocks) + (0 if text_kv is None else 128)
    count = qs.shape[1]
    operands = [qs, *blocks] + ([] if text_kv is None else [text_kv])
    specs = [pl.BlockSpec(memory_space=pltpu.SMEM)] + [vmem()] * len(operands)
    scratch = [
        pltpu.VMEM((keys, 128), BF),
        pltpu.VMEM((keys, 256), BF),
        pltpu.VMEM(held, out_shape.dtype),
    ]
    sems = [pltpu.SemaphoreType.DMA((3,))]
    if before is not None:
        operands.append(keep(before))
        specs.append(hbm())
        scratch.append(pltpu.VMEM(before.shape, before.dtype))
        sems = sems * 2
    return pl.pallas_call(
        kernel,
        out_shape=pltpu.MemorySpace.HBM(out_shape.shape, out_shape.dtype),
        in_specs=specs,
        out_specs=hbm(),
        scratch_shapes=scratch + sems,
        compiler_params=params(24),
        cost_estimate=pl.CostEstimate(
            flops=4 * peers * count * keys * 256,
            bytes_accessed=512 * (peers * count + keys),
            transcendentals=2 * peers * count * keys,
        ),
        name=name,
    )(info, *operands)


def combine_kernel(slots, info, parts_ref, own_hbm, out, grid, own, sem):
    copy = pltpu.make_async_copy(own_hbm, own, sem)
    copy.start()
    o_ref, l_ref = own.at[0], own.at[1]
    members = parts_ref.shape[0]
    block = 128
    count = o_ref.shape[0]
    term = lax.broadcasted_iota(jnp.int32, (STAT_ROWS, 128), 0)
    head = lax.broadcasted_iota(jnp.int32, (STAT_ROWS, 128), 1) // HD
    spread = jnp.where((term // 8 == head) & (term % 8 < 3), 1.0, 0.0).astype(BF)
    frames, tile_h, cells = out.shape[:3]
    tile_w = cells // 16
    copy.wait()
    for place in range(4):
        slot = slots[place]
        rows = pl.ds(pl.multiple_of(slot * block, block), block)
        at = pl.ds(pl.multiple_of(count + slot * STAT_ROWS, STAT_ROWS), STAT_ROWS)
        lses = [l_ref[rows, :]]
        outs = [o_ref[rows, :]]
        for step in range(1, members):
            member = jnp.bitwise_xor(info[3], step)
            lses.append(
                lax.dot_general(
                    parts_ref[member, at, :],
                    spread,
                    (((0,), (0,)), ((), ())),
                    preferred_element_type=F32,
                )
            )
            outs.append(parts_ref[member, rows, :].astype(F32))
        top = functools.reduce(jnp.maximum, lses)
        shares = [jnp.exp2(lse - top) for lse in lses]
        weighted = sum(share * part for share, part in zip(shares, outs))
        merged = weighted / sum(shares)
        at = 0
        for far in range(4):
            for frame in range(frames):
                for row in range(tile_h):
                    first = (far * 4 + place) * tile_w
                    grid[frame, row, first : first + tile_w, :] = merged[at : at + tile_w]
                    at += tile_w
    out[...] = grid[...].astype(BF)


def combine(slots, info, parts, own, shape):
    smem = pl.BlockSpec(memory_space=pltpu.SMEM)
    return pl.pallas_call(
        combine_kernel,
        out_shape=jax.ShapeDtypeStruct(shape, BF),
        in_specs=[smem, smem, vmem(), hbm()],
        out_specs=vmem(),
        scratch_shapes=[
            pltpu.VMEM(shape, F32),
            pltpu.VMEM(own.shape, F32),
            pltpu.SemaphoreType.DMA,
        ],
        compiler_params=params(8),
        name="combine",
    )(slots, info, parts, keep(own))


def on_device(latents, prompt_rows, peg_weight, modulation_weight, qkv_weight, text_len, timestep):
    frames, tile_h, tile_w, width = latents.shape[1:]
    head_width = qkv_weight.shape[2]
    zl_at = lax.axis_index("zl")
    x_at = lax.axis_index("x")
    member = lax.axis_index("v") * 2 + zl_at

    row_axes = ("u", "v", "zl")
    padded = with_halo(latents, ((row_axes, 2),), 1)
    padded, peg_weight, modulation_weight = lax.optimization_barrier(
        (padded, peg_weight, modulation_weight)
    )
    padded = with_halo(padded, ((("zh", "x"), 3),), 1)
    shard = qkv_weight.reshape(qkv_weight.shape[0], 3 * head_width)
    weight = lax.all_gather(shard, ("item",) + row_axes, axis=0, tiled=True)
    summed = latents.astype(F32)
    for row_tap in range(3):
        for col_tap in range(3):
            summed = summed + padded[
                :, :, row_tap : row_tap + tile_h, col_tap : col_tap + tile_w, :
            ].astype(F32) * peg_weight[row_tap, col_tap].astype(F32)
    peg = summed.astype(BF).reshape(frames * tile_h * tile_w, width)

    activation = jax.nn.silu(time_angles(timestep[0], modulation_weight.shape[0])).astype(BF)
    own_columns = jnp.dot(activation[None, :], modulation_weight, preferred_element_type=F32)
    rest = own_columns.reshape(3, 128)
    terms = []
    for _ in range(3):
        terms.append(lax.reduce_precision(rest, 8, 7))
        rest = rest - terms[-1]
    extra = jnp.concatenate(terms).astype(BF)
    extra = jnp.pad(extra, ((0, peg.shape[0] - 9), (0, 0)))
    peg = jnp.concatenate([peg, extra], axis=1)

    tokens = lax.all_gather(peg, "zh", axis=0, tiled=True)
    half = tokens.shape[0] // 2
    low, high = tokens[:half], tokens[half:]
    up = [(i, (i + 1) % 4) for i in range(4)]
    down = [(i, (i - 1) % 4) for i in range(4)]
    a0, b1 = lax.ppermute(low, "x", up), lax.ppermute(high, "x", down)
    a1, b0 = lax.ppermute(high, "x", up), lax.ppermute(low, "x", down)
    a0, b1 = lax.optimization_barrier((a0, b1))
    c0, c1 = lax.ppermute(a0, "x", up), lax.ppermute(b1, "x", down)
    pieces = (low, high, a0, a1, b0, b1, c0, c1)
    distance = (jnp.arange(4, dtype=jnp.int32) - x_at) % 4
    slots = jnp.where(distance == 0, 0, jnp.where(distance == 3, 1, distance + 1))

    lower = member * TEXT_PART
    start = jnp.minimum(lower, prompt_rows.shape[1] - TEXT_PART)
    text_rows = lax.dynamic_slice_in_dim(prompt_rows[0], start, TEXT_PART, axis=0)
    queries, kv, text_kv = project(slots, pieces, text_rows, weight)
    group = ("v", "zl")
    qs = lax.all_to_all(queries, group, split_axis=0, concat_axis=0, tiled=True)
    near = [lax.ppermute(kv, "u", up), lax.ppermute(kv, "u", down)]
    near = lax.optimization_barrier(near)
    count = kv.shape[0]
    far = [
        lax.ppermute(near[0][: count // 2], "u", up),
        lax.ppermute(near[1][count // 2 :], "u", down),
    ]
    info = jnp.stack([start, lower, text_len[0], member])
    shape = (3, 2, count, 128)
    first = jax.ShapeDtypeStruct(shape, F32)
    first = attend(first_kernel, "first", 3, first, shape, info, qs, [kv, *near], text_kv)
    shape = (4, count + count // 128 * STAT_ROWS, 128)
    parts = jax.ShapeDtypeStruct(shape, BF)
    parts = attend(rest_kernel, "rest", 3, parts, (3,) + shape[1:], info, qs, far, None, first)
    parts = lax.all_to_all(parts, group, split_axis=0, concat_axis=0, tiled=True)
    shape = (2, count, 128)
    own = jax.ShapeDtypeStruct(shape, F32)
    own = attend(own_kernel, "own", 1, own, shape, info, qs, [kv, *near, *far], text_kv)
    shape = (frames, tile_h, 16 * tile_w, head_width)
    return combine(slots, info, parts, own, shape)[None]


def solution(mesh):
    fine = Mesh(mesh.devices.reshape(2, 4, 2, 2, 4, 4), ("item", "u", "v", "zl", "zh", "x"))
    row = ("u", "v", "zl")
    col = ("zh", "x")
    in_specs = (
        P("item", None, row, col, None),
        P("item", None, None),
        P(),
        P(None, col),
        P(("item",) + row, None, col),
        P("item"),
        P("item"),
    )
    out_specs = P("item", None, row, None, col)
    return jax.shard_map(
        on_device, mesh=fine, in_specs=in_specs, out_specs=out_specs, check_vma=False
    )
```

```python
import functools
import math

import jax
import jax.numpy as jnp
from jax import lax
from jax.experimental import pallas as pl
from jax.experimental.pallas import tpu as pltpu
from jax.sharding import Mesh, PartitionSpec as P

HD = 64
LOG2E = 1.4426950408889634
SCALE2 = 0.125 * LOG2E
BF = jnp.bfloat16
F32 = jnp.float32
TEXT_PART = 64
STAT_ROWS = 16


def vmem(*shape):
    return pl.BlockSpec(memory_space=pltpu.VMEM)


def hbm():
    return pl.BlockSpec(memory_space=pltpu.MemorySpace.HBM)


def keep(x):
    return pltpu.with_memory_space_constraint(x, pltpu.MemorySpace.HBM)


def params(mib):
    return pltpu.CompilerParams(vmem_limit_bytes=mib << 20)


def with_halo(block, sides, width):
    for axis, dim in sides:
        count = lax.axis_size(axis)
        forward = [(i, i + 1) for i in range(count - 1)]
        backward = [(target, source) for source, target in forward]
        low = lax.ppermute(
            lax.slice_in_dim(block, block.shape[dim] - width, None, axis=dim), axis, forward
        )
        high = lax.ppermute(lax.slice_in_dim(block, 0, width, axis=dim), axis, backward)
        block = jnp.concatenate([low, block, high], axis=dim)
    return block


def time_angles(step, count):
    half = count // 2
    freqs = jnp.exp(-math.log(10000.0) * jnp.arange(half, dtype=F32) / half)
    angle = step.astype(F32) * freqs
    return jnp.concatenate([jnp.cos(angle), jnp.sin(angle)])


def project_kernel(
    slots, x0, x1, a0, a1, b0, b1, c0, c1, text, w_hbm,
    q_out, kv_out, text_out,
    held, mod, extra, normed, w_ref, in_sems, w_sem,
):
    half = x0.shape[0]
    rows = 2 * half
    width = text.shape[1]
    tile = rows // 4
    arrived = []
    for slot, (low, high) in enumerate(((x0, x1), (a0, a1), (b0, b1), (c0, c1))):
        arrived += [(low, slot * rows), (high, slot * rows + half)]

    def tail(i):
        piece, at = arrived[i]
        size = piece.shape[0]
        return pltpu.make_async_copy(
            piece.at[:, pl.ds(width, 128)], extra.at[pl.ds(at, size), :], in_sems.at[0, i]
        )

    def body(i):
        piece, at = arrived[i]
        size = piece.shape[0]
        return pltpu.make_async_copy(
            piece.at[:, pl.ds(0, width)], held.at[pl.ds(at, size), :], in_sems.at[1, i]
        )

    count = len(arrived)
    for i in range(count):
        tail(i).start()
    for i in range(count):
        body(i).start()
    fetch = pltpu.make_async_copy(w_hbm, w_ref, w_sem)
    fetch.start()
    for i in range(count):
        tail(i).wait()
    for place in range(4):
        base = pl.multiple_of(slots[place] * rows, rows)
        terms = extra[pl.ds(base, rows), :].astype(F32)
        for far in range(4):
            for chunk in range(3):
                at = (far * 4 + place) * 3 + chunk
                kind, first = divmod(at * 128, width)
                row = far * tile + chunk
                mod[kind : kind + 1, first : first + 128] = (
                    terms[row : row + 1] + terms[row + 3 : row + 4] + terms[row + 6 : row + 7]
                )
    shift = mod[0:1, :]
    gain = 1.0 + mod[1:2, :]

    def norm(rows_in, at):
        values = rows_in.astype(F32)
        center = jnp.sum(values, axis=1, keepdims=True) * (1.0 / width)
        centered = values - center
        spread = jnp.sum(centered * centered, axis=1, keepdims=True) * (1.0 / width)
        result = centered * lax.rsqrt(spread + 1e-06) * gain + shift
        normed[at : at + rows_in.shape[0], :] = result.astype(BF)

    norm(text[...], 4 * rows)
    for part in range(2):
        first = 2 * rows * part
        for i in range(count):
            if first <= arrived[i][1] < first + 2 * rows:
                body(i).wait()
        for block in (2 * part, 2 * part + 1):
            norm(held[block * rows : (block + 1) * rows, :], block * rows)
        last = first + 2 * rows + (text.shape[0] if part else 0)
        if part == 0:
            fetch.wait()
        out = jnp.dot(normed[first:last, :], w_ref[...], preferred_element_type=F32).astype(BF)
        span = pl.ds(first, 2 * rows)
        q_out[span, :] = out[: 2 * rows, :128]
        kv_out[span, :] = out[: 2 * rows, 128:]
        if part:
            text_out[...] = out[2 * rows :, 128:]


def project(slots, pieces, text, weight):
    half, lanes = pieces[0].shape
    rows = 2 * half
    width = text.shape[1]
    return pl.pallas_call(
        project_kernel,
        out_shape=[
            jax.ShapeDtypeStruct((4 * rows, 128), BF),
            jax.ShapeDtypeStruct((4 * rows, 256), BF),
            jax.ShapeDtypeStruct((text.shape[0], 256), BF),
        ],
        in_specs=[pl.BlockSpec(memory_space=pltpu.SMEM)] + [hbm()] * 8 + [vmem(), hbm()],
        out_specs=[vmem()] * 3,
        scratch_shapes=[
            pltpu.VMEM((4 * rows, width), BF),
            pltpu.VMEM((2, width), F32),
            pltpu.VMEM((4 * rows, 128), BF),
            pltpu.VMEM((4 * rows + text.shape[0], width), BF),
            pltpu.VMEM(weight.shape, BF),
            pltpu.SemaphoreType.DMA((2, 8)),
            pltpu.SemaphoreType.DMA,
        ],
        compiler_params=params(28),
        cost_estimate=pl.CostEstimate(
            flops=8 * rows * width * weight.shape[1],
            bytes_accessed=2 * (4 * rows * lanes + weight.size),
            transcendentals=4 * rows,
        ),
        name="project",
    )(slots, *map(keep, pieces), text, keep(weight))


def load_keys(blocks, text_kv, keys, values):
    at = 0
    for block in blocks:
        size = block.shape[0]
        keys[at : at + size, :] = block[:, :128]
        values[at : at + size, :128] = block[:, 128:]
        at += size
    if text_kv is not None:
        pad = 128 - TEXT_PART
        keys[at : at + TEXT_PART, :] = text_kv[:, :128]
        keys[at + TEXT_PART :, :] = jnp.zeros((pad, 128), BF)
        values[at : at + TEXT_PART, :128] = text_kv[:, 128:]
        values[at + TEXT_PART :, :128] = jnp.zeros((pad, 128), BF)
    values[:, 128:] = jnp.ones((values.shape[0], 128), BF)


def softmax_block(info, q, keys, values, has_text):
    rows = q.shape[0]
    latent = keys.shape[0] - (128 if has_text else 0)
    lane = lax.broadcasted_iota(jnp.int32, (rows, 128), 1)
    position = info[0] + lane
    valid = (position >= info[1]) & (position < info[2]) & (lane < TEXT_PART)
    q = q.astype(F32)
    accs, tops = [], []
    for head in range(2):
        own = jnp.where(lane // HD == head, q, 0.0).astype(BF)
        s = lax.dot_general(
            own, keys[...], (((1,), (1,)), ((), ())), preferred_element_type=F32
        )
        top = jnp.max(s[:, :latent], axis=1, keepdims=True)
        if has_text:
            text = jnp.where(valid, s[:, latent:], -1e30)
            top = jnp.maximum(top, jnp.max(text, axis=1, keepdims=True))
        top = top * SCALE2
        p = jnp.exp2(s[:, :latent] * SCALE2 - top).astype(BF)
        if has_text:
            p_text = jnp.where(valid, jnp.exp2(text * SCALE2 - top), 0.0).astype(BF)
            p = jnp.concatenate([p, p_text], axis=1)
        accs.append(jnp.dot(p, values[...], preferred_element_type=F32))
        tops.append(top)
    total = jnp.where(lane < HD, accs[0][:, 128:], accs[1][:, 128:])
    weighted = jnp.where(lane < HD, accs[0][:, :128], accs[1][:, :128])
    return weighted / total, jnp.where(lane < HD, tops[0], tops[1]) + jnp.log(total) * LOG2E


def first_kernel(info, q1, q23, kv0, kv1, kv2, text_kv, o_ref, keys, values, held, sems):
    load_keys((kv0, kv1, kv2), text_kv, keys, values)
    sends = []
    for i, q in enumerate((q1[...], q23[0], q23[1])):
        held[i, 0], held[i, 1] = softmax_block(info, q, keys, values, True)
        sends.append(pltpu.make_async_copy(held.at[i], o_ref.at[i], sems.at[i]))
        sends[-1].start()
    for send in sends:
        send.wait()


def rest_kernel(
    info, q1, q23, kv3, kv4, before_hbm, o_ref, keys, values, held, before, sems, in_sems
):
    fetches = [
        pltpu.make_async_copy(before_hbm.at[i], before.at[i], in_sems.at[i]) for i in range(3)
    ]
    for fetch in fetches:
        fetch.start()
    count = q1.shape[0]
    load_keys((kv3, kv4), None, keys, values)
    term = lax.broadcasted_iota(jnp.int32, (STAT_ROWS, 128), 0)
    lane = lax.broadcasted_iota(jnp.int32, (STAT_ROWS, 128), 1)
    sends = []
    for i, q in enumerate((q1[...], q23[0], q23[1])):
        member = jnp.bitwise_xor(info[3], i + 1)
        out, lse = softmax_block(info, q, keys, values, False)
        fetches[i].wait()
        earlier = before[i, 1]
        top = jnp.maximum(lse, earlier)
        new, old = jnp.exp2(lse - top), jnp.exp2(earlier - top)
        total = new + old
        held[i, :count, :] = ((new * out + old * before[i, 0]) / total).astype(BF)
        lse = top + jnp.log(total) * LOG2E
        across = jnp.zeros((STAT_ROWS, count), F32)
        for part in range(3):
            piece = lse.astype(BF)
            lse = lse - piece.astype(F32)
            pick = jnp.where((term % 8 == part) & (lane == term // 8 * HD), 1.0, 0.0).astype(BF)
            across = across + lax.dot_general(
                pick, piece, (((1,), (1,)), ((), ())), preferred_element_type=F32
            )
        for tile in range(count // 128):
            at = count + tile * STAT_ROWS
            held[i, at : at + STAT_ROWS, :] = across[:, tile * 128 : (tile + 1) * 128].astype(BF)
        sends.append(pltpu.make_async_copy(held.at[i], o_ref.at[member], sems.at[i]))
        sends[-1].start()
    for send in sends:
        send.wait()


def own_kernel(info, q_ref, kv0, kv1, kv2, kv3, kv4, text_kv, o_ref, keys, values, held, sems):
    load_keys((kv0, kv1, kv2, kv3, kv4), text_kv, keys, values)
    held[0], held[1] = softmax_block(info, q_ref[...], keys, values, True)
    copy = pltpu.make_async_copy(held, o_ref, sems.at[0])
    copy.start()
    copy.wait()


def attend(kernel, name, peers, out_shape, held, info, qs, blocks, text_kv=None, before=None):
    keys = sum(block.shape[0] for block in blocks) + (0 if text_kv is None else 128)
    count = qs[0].shape[0]
    operands = [*qs, *blocks] + ([] if text_kv is None else [text_kv])
    specs = [pl.BlockSpec(memory_space=pltpu.SMEM)] + [vmem()] * len(operands)
    scratch = [
        pltpu.VMEM((keys, 128), BF),
        pltpu.VMEM((keys, 256), BF),
        pltpu.VMEM(held, out_shape.dtype),
    ]
    sems = [pltpu.SemaphoreType.DMA((3,))]
    if before is not None:
        operands.append(keep(before))
        specs.append(hbm())
        scratch.append(pltpu.VMEM(before.shape, before.dtype))
        sems = sems * 2
    return pl.pallas_call(
        kernel,
        out_shape=pltpu.MemorySpace.HBM(out_shape.shape, out_shape.dtype),
        in_specs=specs,
        out_specs=hbm(),
        scratch_shapes=scratch + sems,
        compiler_params=params(24),
        cost_estimate=pl.CostEstimate(
            flops=4 * peers * count * keys * 256,
            bytes_accessed=512 * (peers * count + keys),
            transcendentals=2 * peers * count * keys,
        ),
        name=name,
    )(info, *operands)


def combine_kernel(slots, info, parts_ref, own_hbm, out, grid, own, sem):
    copy = pltpu.make_async_copy(own_hbm, own, sem)
    copy.start()
    o_ref, l_ref = own.at[0], own.at[1]
    members = parts_ref.shape[0]
    block = 128
    count = o_ref.shape[0]
    term = lax.broadcasted_iota(jnp.int32, (STAT_ROWS, 128), 0)
    head = lax.broadcasted_iota(jnp.int32, (STAT_ROWS, 128), 1) // HD
    spread = jnp.where((term // 8 == head) & (term % 8 < 3), 1.0, 0.0).astype(BF)
    frames, tile_h, cells = out.shape[:3]
    tile_w = cells // 16
    copy.wait()
    for place in range(4):
        slot = slots[place]
        rows = pl.ds(pl.multiple_of(slot * block, block), block)
        at = pl.ds(pl.multiple_of(count + slot * STAT_ROWS, STAT_ROWS), STAT_ROWS)
        lses = [l_ref[rows, :]]
        outs = [o_ref[rows, :]]
        for step in range(1, members):
            member = jnp.bitwise_xor(info[3], step)
            lses.append(
                lax.dot_general(
                    parts_ref[member, at, :],
                    spread,
                    (((0,), (0,)), ((), ())),
                    preferred_element_type=F32,
                )
            )
            outs.append(parts_ref[member, rows, :].astype(F32))
        top = functools.reduce(jnp.maximum, lses)
        shares = [jnp.exp2(lse - top) for lse in lses]
        weighted = sum(share * part for share, part in zip(shares, outs))
        merged = weighted / sum(shares)
        at = 0
        for far in range(4):
            for frame in range(frames):
                for row in range(tile_h):
                    first = (far * 4 + place) * tile_w
                    grid[frame, row, first : first + tile_w, :] = merged[at : at + tile_w]
                    at += tile_w
    out[...] = grid[...].astype(BF)


def combine(slots, info, parts, own, shape):
    smem = pl.BlockSpec(memory_space=pltpu.SMEM)
    return pl.pallas_call(
        combine_kernel,
        out_shape=jax.ShapeDtypeStruct(shape, BF),
        in_specs=[smem, smem, vmem(), hbm()],
        out_specs=vmem(),
        scratch_shapes=[
            pltpu.VMEM(shape, F32),
            pltpu.VMEM(own.shape, F32),
            pltpu.SemaphoreType.DMA,
        ],
        compiler_params=params(8),
        name="combine",
    )(slots, info, parts, keep(own))


def on_device(latents, prompt_rows, peg_weight, modulation_weight, qkv_weight, text_len, timestep):
    frames, tile_h, tile_w, width = latents.shape[1:]
    head_width = qkv_weight.shape[2]
    zl_at = lax.axis_index("zl")
    x_at = lax.axis_index("x")
    member = lax.axis_index("v") * 2 + zl_at

    row_axes = ("u", "v", "zl")
    padded = with_halo(latents, ((row_axes, 2),), 1)
    padded, peg_weight, modulation_weight = lax.optimization_barrier(
        (padded, peg_weight, modulation_weight)
    )
    padded = with_halo(padded, ((("zh", "x"), 3),), 1)
    shard = qkv_weight.reshape(qkv_weight.shape[0], 3 * head_width)
    weight = lax.all_gather(shard, ("item",) + row_axes, axis=0, tiled=True)
    summed = latents.astype(F32)
    for row_tap in range(3):
        for col_tap in range(3):
            summed = summed + padded[
                :, :, row_tap : row_tap + tile_h, col_tap : col_tap + tile_w, :
            ].astype(F32) * peg_weight[row_tap, col_tap].astype(F32)
    peg = summed.astype(BF).reshape(frames * tile_h * tile_w, width)

    activation = jax.nn.silu(time_angles(timestep[0], modulation_weight.shape[0])).astype(BF)
    own_columns = jnp.dot(activation[None, :], modulation_weight, preferred_element_type=F32)
    rest = own_columns.reshape(3, 128)
    terms = []
    for _ in range(3):
        terms.append(lax.reduce_precision(rest, 8, 7))
        rest = rest - terms[-1]
    extra = jnp.concatenate(terms).astype(BF)
    extra = jnp.pad(extra, ((0, peg.shape[0] - 9), (0, 0)))
    peg = jnp.concatenate([peg, extra], axis=1)

    tokens = lax.all_gather(peg, "zh", axis=0, tiled=True)
    half = tokens.shape[0] // 2
    low, high = tokens[:half], tokens[half:]
    up = [(i, (i + 1) % 4) for i in range(4)]
    down = [(i, (i - 1) % 4) for i in range(4)]
    a0, b1 = lax.ppermute(low, "x", up), lax.ppermute(high, "x", down)
    a1, b0 = lax.ppermute(high, "x", up), lax.ppermute(low, "x", down)
    a0, b1 = lax.optimization_barrier((a0, b1))
    c0, c1 = lax.ppermute(a0, "x", up), lax.ppermute(b1, "x", down)
    pieces = (low, high, a0, a1, b0, b1, c0, c1)
    distance = (jnp.arange(4, dtype=jnp.int32) - x_at) % 4
    slots = jnp.where(distance == 0, 0, jnp.where(distance == 3, 1, distance + 1))

    lower = member * TEXT_PART
    start = jnp.minimum(lower, prompt_rows.shape[1] - TEXT_PART)
    text_rows = lax.dynamic_slice_in_dim(prompt_rows[0], start, TEXT_PART, axis=0)
    queries, kv, text_kv = project(slots, pieces, text_rows, weight)
    group = ("v", "zl")
    swap = [(0, 1), (1, 0)]
    beside = lax.ppermute(queries, "zl", swap)
    across = lax.ppermute(jnp.stack([queries, beside]), "v", swap)
    qs = [beside, across]
    near = [lax.ppermute(kv, "u", up), lax.ppermute(kv, "u", down)]
    near = lax.optimization_barrier(near)
    count = kv.shape[0]
    far = [
        lax.ppermute(near[0][: count // 2], "u", up),
        lax.ppermute(near[1][count // 2 :], "u", down),
    ]
    info = jnp.stack([start, lower, text_len[0], member])
    shape = (3, 2, count, 128)
    first = jax.ShapeDtypeStruct(shape, F32)
    first = attend(first_kernel, "first", 3, first, shape, info, qs, [kv, *near], text_kv)
    shape = (4, count + count // 128 * STAT_ROWS, 128)
    parts = jax.ShapeDtypeStruct(shape, BF)
    parts = attend(rest_kernel, "rest", 3, parts, (3,) + shape[1:], info, qs, far, None, first)
    parts = lax.all_to_all(parts, group, split_axis=0, concat_axis=0, tiled=True)
    shape = (2, count, 128)
    own = jax.ShapeDtypeStruct(shape, F32)
    own = attend(own_kernel, "own", 1, own, shape, info, [queries], [kv, *near, *far], text_kv)
    shape = (frames, tile_h, 16 * tile_w, head_width)
    return combine(slots, info, parts, own, shape)[None]


def solution(mesh):
    fine = Mesh(mesh.devices.reshape(2, 4, 2, 2, 4, 4), ("item", "u", "v", "zl", "zh", "x"))
    row = ("u", "v", "zl")
    col = ("zh", "x")
    in_specs = (
        P("item", None, row, col, None),
        P("item", None, None),
        P(),
        P(None, col),
        P(("item",) + row, None, col),
        P("item"),
        P("item"),
    )
    out_specs = P("item", None, row, None, col)
    return jax.shard_map(
        on_device, mesh=fine, in_specs=in_specs, out_specs=out_specs, check_vma=False
    )
```

```python
import functools
import math

import jax
import jax.numpy as jnp
from jax import lax
from jax.experimental import pallas as pl
from jax.experimental.pallas import tpu as pltpu
from jax.sharding import Mesh, PartitionSpec as P

HD = 64
LOG2E = 1.4426950408889634
SCALE2 = 0.125 * LOG2E
BF = jnp.bfloat16
F32 = jnp.float32
TEXT_PART = 64
STAT_ROWS = 16


def vmem(*shape):
    return pl.BlockSpec(memory_space=pltpu.VMEM)


def hbm():
    return pl.BlockSpec(memory_space=pltpu.MemorySpace.HBM)


def keep(x):
    return pltpu.with_memory_space_constraint(x, pltpu.MemorySpace.HBM)


def params(mib):
    return pltpu.CompilerParams(vmem_limit_bytes=mib << 20)


def with_halo(block, sides, width):
    for axis, dim in sides:
        count = lax.axis_size(axis)
        forward = [(i, i + 1) for i in range(count - 1)]
        backward = [(target, source) for source, target in forward]
        low = lax.ppermute(
            lax.slice_in_dim(block, block.shape[dim] - width, None, axis=dim), axis, forward
        )
        high = lax.ppermute(lax.slice_in_dim(block, 0, width, axis=dim), axis, backward)
        block = jnp.concatenate([low, block, high], axis=dim)
    return block


def time_angles(step, count):
    half = count // 2
    freqs = jnp.exp(-math.log(10000.0) * jnp.arange(half, dtype=F32) / half)
    angle = step.astype(F32) * freqs
    return jnp.concatenate([jnp.cos(angle), jnp.sin(angle)])


def project_kernel(
    slots, x0, x1, a0, a1, b0, b1, c0, c1, text, w_hbm,
    q_out, kv_out, text_out,
    held, mod, extra, normed, w_ref, in_sems, w_sem,
):
    half = x0.shape[0]
    rows = 2 * half
    width = text.shape[1]
    tile = rows // 4
    arrived = []
    for slot, (low, high) in enumerate(((x0, x1), (a0, a1), (b0, b1), (c0, c1))):
        arrived += [(low, slot * rows), (high, slot * rows + half)]

    def tail(i):
        piece, at = arrived[i]
        size = piece.shape[0]
        return pltpu.make_async_copy(
            piece.at[:, pl.ds(width, 128)], extra.at[pl.ds(at, size), :], in_sems.at[0, i]
        )

    def body(i):
        piece, at = arrived[i]
        size = piece.shape[0]
        return pltpu.make_async_copy(
            piece.at[:, pl.ds(0, width)], held.at[pl.ds(at, size), :], in_sems.at[1, i]
        )

    count = len(arrived)
    for i in range(count):
        tail(i).start()
    for i in range(count):
        body(i).start()
    fetch = pltpu.make_async_copy(w_hbm, w_ref, w_sem)
    fetch.start()
    for i in range(count):
        tail(i).wait()
    for place in range(4):
        base = pl.multiple_of(slots[place] * rows, rows)
        terms = extra[pl.ds(base, rows), :].astype(F32)
        for far in range(4):
            for chunk in range(3):
                at = (far * 4 + place) * 3 + chunk
                kind, first = divmod(at * 128, width)
                row = far * tile + chunk
                mod[kind : kind + 1, first : first + 128] = (
                    terms[row : row + 1] + terms[row + 3 : row + 4] + terms[row + 6 : row + 7]
                )
    shift = mod[0:1, :]
    gain = 1.0 + mod[1:2, :]

    def norm(rows_in, at):
        values = rows_in.astype(F32)
        center = jnp.sum(values, axis=1, keepdims=True) * (1.0 / width)
        centered = values - center
        spread = jnp.sum(centered * centered, axis=1, keepdims=True) * (1.0 / width)
        result = centered * lax.rsqrt(spread + 1e-06) * gain + shift
        normed[at : at + rows_in.shape[0], :] = result.astype(BF)

    norm(text[...], 4 * rows)
    for part in range(2):
        first = 2 * rows * part
        for i in range(count):
            if first <= arrived[i][1] < first + 2 * rows:
                body(i).wait()
        for block in (2 * part, 2 * part + 1):
            norm(held[block * rows : (block + 1) * rows, :], block * rows)
        last = first + 2 * rows + (text.shape[0] if part else 0)
        if part == 0:
            fetch.wait()
        out = jnp.dot(normed[first:last, :], w_ref[...], preferred_element_type=F32).astype(BF)
        span = pl.ds(first, 2 * rows)
        q_out[span, :] = out[: 2 * rows, :128]
        kv_out[span, :] = out[: 2 * rows, 128:]
        if part:
            text_out[...] = out[2 * rows :, 128:]


def project(slots, pieces, text, weight):
    half, lanes = pieces[0].shape
    rows = 2 * half
    width = text.shape[1]
    return pl.pallas_call(
        project_kernel,
        out_shape=[
            jax.ShapeDtypeStruct((4 * rows, 128), BF),
            jax.ShapeDtypeStruct((4 * rows, 256), BF),
            jax.ShapeDtypeStruct((text.shape[0], 256), BF),
        ],
        in_specs=[pl.BlockSpec(memory_space=pltpu.SMEM)] + [hbm()] * 8 + [vmem(), hbm()],
        out_specs=[vmem()] * 3,
        scratch_shapes=[
            pltpu.VMEM((4 * rows, width), BF),
            pltpu.VMEM((2, width), F32),
            pltpu.VMEM((4 * rows, 128), BF),
            pltpu.VMEM((4 * rows + text.shape[0], width), BF),
            pltpu.VMEM(weight.shape, BF),
            pltpu.SemaphoreType.DMA((2, 8)),
            pltpu.SemaphoreType.DMA,
        ],
        compiler_params=params(28),
        cost_estimate=pl.CostEstimate(
            flops=8 * rows * width * weight.shape[1],
            bytes_accessed=2 * (4 * rows * lanes + weight.size),
            transcendentals=4 * rows,
        ),
        name="project",
    )(slots, *map(keep, pieces), text, keep(weight))


def load_keys(blocks, text_kv, keys, values):
    at = 0
    for block in blocks:
        size = block.shape[0]
        keys[at : at + size, :] = block[:, :128]
        values[at : at + size, :128] = block[:, 128:]
        at += size
    if text_kv is not None:
        pad = 128 - TEXT_PART
        keys[at : at + TEXT_PART, :] = text_kv[:, :128]
        keys[at + TEXT_PART :, :] = jnp.zeros((pad, 128), BF)
        values[at : at + TEXT_PART, :128] = text_kv[:, 128:]
        values[at + TEXT_PART :, :128] = jnp.zeros((pad, 128), BF)
    values[:, 128:] = jnp.ones((values.shape[0], 128), BF)


def softmax_block(info, q, keys, values, has_text):
    rows = q.shape[0]
    latent = keys.shape[0] - (128 if has_text else 0)
    lane = lax.broadcasted_iota(jnp.int32, (rows, 128), 1)
    position = info[0] + lane
    valid = (position >= info[1]) & (position < info[2]) & (lane < TEXT_PART)
    q = q.astype(F32)
    accs, tops = [], []
    for head in range(2):
        own = jnp.where(lane // HD == head, q, 0.0).astype(BF)
        s = lax.dot_general(
            own, keys[...], (((1,), (1,)), ((), ())), preferred_element_type=F32
        )
        top = jnp.max(s[:, :latent], axis=1, keepdims=True)
        if has_text:
            text = jnp.where(valid, s[:, latent:], -1e30)
            top = jnp.maximum(top, jnp.max(text, axis=1, keepdims=True))
        top = top * SCALE2
        p = jnp.exp2(s[:, :latent] * SCALE2 - top).astype(BF)
        if has_text:
            p_text = jnp.where(valid, jnp.exp2(text * SCALE2 - top), 0.0).astype(BF)
            p = jnp.concatenate([p, p_text], axis=1)
        accs.append(jnp.dot(p, values[...], preferred_element_type=F32))
        tops.append(top)
    total = jnp.where(lane < HD, accs[0][:, 128:], accs[1][:, 128:])
    weighted = jnp.where(lane < HD, accs[0][:, :128], accs[1][:, :128])
    return weighted / total, jnp.where(lane < HD, tops[0], tops[1]) + jnp.log(total) * LOG2E


def first_kernel(info, q1, q2, q3, kv0, kv1, kv2, text_kv, o_ref, keys, values):
    load_keys((kv0, kv1, kv2), text_kv, keys, values)
    for i, q_ref in enumerate((q1, q2, q3)):
        o_ref[i, 0], o_ref[i, 1] = softmax_block(info, q_ref[...], keys, values, True)


def rest_kernel(
    info, q1, q2, q3, kv3, kv4, before, o_ref, keys, values, held, sems
):
    count = q1.shape[0]
    load_keys((kv3, kv4), None, keys, values)
    term = lax.broadcasted_iota(jnp.int32, (STAT_ROWS, 128), 0)
    lane = lax.broadcasted_iota(jnp.int32, (STAT_ROWS, 128), 1)
    sends = []
    for i, q_ref in enumerate((q1, q2, q3)):
        member = jnp.bitwise_xor(info[3], i + 1)
        out, lse = softmax_block(info, q_ref[...], keys, values, False)
        earlier = before[i, 1]
        top = jnp.maximum(lse, earlier)
        new, old = jnp.exp2(lse - top), jnp.exp2(earlier - top)
        total = new + old
        held[i, :count, :] = ((new * out + old * before[i, 0]) / total).astype(BF)
        lse = top + jnp.log(total) * LOG2E
        across = jnp.zeros((STAT_ROWS, count), F32)
        for part in range(3):
            piece = lse.astype(BF)
            lse = lse - piece.astype(F32)
            pick = jnp.where((term % 8 == part) & (lane == term // 8 * HD), 1.0, 0.0).astype(BF)
            across = across + lax.dot_general(
                pick, piece, (((1,), (1,)), ((), ())), preferred_element_type=F32
            )
        for tile in range(count // 128):
            at = count + tile * STAT_ROWS
            held[i, at : at + STAT_ROWS, :] = across[:, tile * 128 : (tile + 1) * 128].astype(BF)
        sends.append(pltpu.make_async_copy(held.at[i], o_ref.at[member], sems.at[i]))
        sends[-1].start()
    for send in sends:
        send.wait()


def own_kernel(info, q_ref, kv0, kv1, kv2, kv3, kv4, text_kv, o_ref, keys, values, held, sems):
    load_keys((kv0, kv1, kv2, kv3, kv4), text_kv, keys, values)
    held[0], held[1] = softmax_block(info, q_ref[...], keys, values, True)
    copy = pltpu.make_async_copy(held, o_ref, sems.at[0])
    copy.start()
    copy.wait()


def attend(kernel, name, peers, out_shape, held, info, qs, blocks, text_kv=None, before=None):
    keys = sum(block.shape[0] for block in blocks) + (0 if text_kv is None else 128)
    count = qs[0].shape[0]
    operands = [*qs, *blocks] + [x for x in (text_kv, before) if x is not None]
    scratch = [pltpu.VMEM((keys, 128), BF), pltpu.VMEM((keys, 256), BF)]
    out_spec = vmem()
    if held is not None:
        scratch += [pltpu.VMEM(held, out_shape.dtype), pltpu.SemaphoreType.DMA((3,))]
        out_shape, out_spec = pltpu.MemorySpace.HBM(out_shape.shape, out_shape.dtype), hbm()
    return pl.pallas_call(
        kernel,
        out_shape=out_shape,
        in_specs=[pl.BlockSpec(memory_space=pltpu.SMEM)] + [vmem()] * len(operands),
        out_specs=out_spec,
        scratch_shapes=scratch,
        compiler_params=params(24),
        cost_estimate=pl.CostEstimate(
            flops=4 * peers * count * keys * 256,
            bytes_accessed=512 * (peers * count + keys),
            transcendentals=2 * peers * count * keys,
        ),
        name=name,
    )(info, *operands)


def combine_kernel(slots, info, parts_ref, own_hbm, out, grid, own, sem):
    copy = pltpu.make_async_copy(own_hbm, own, sem)
    copy.start()
    o_ref, l_ref = own.at[0], own.at[1]
    members = parts_ref.shape[0]
    block = 128
    count = o_ref.shape[0]
    term = lax.broadcasted_iota(jnp.int32, (STAT_ROWS, 128), 0)
    head = lax.broadcasted_iota(jnp.int32, (STAT_ROWS, 128), 1) // HD
    spread = jnp.where((term // 8 == head) & (term % 8 < 3), 1.0, 0.0).astype(BF)
    frames, tile_h, cells = out.shape[:3]
    tile_w = cells // 16
    copy.wait()
    for place in range(4):
        slot = slots[place]
        rows = pl.ds(pl.multiple_of(slot * block, block), block)
        at = pl.ds(pl.multiple_of(count + slot * STAT_ROWS, STAT_ROWS), STAT_ROWS)
        lses = [l_ref[rows, :]]
        outs = [o_ref[rows, :]]
        for step in range(1, members):
            member = jnp.bitwise_xor(info[3], step)
            lses.append(
                lax.dot_general(
                    parts_ref[member, at, :],
                    spread,
                    (((0,), (0,)), ((), ())),
                    preferred_element_type=F32,
                )
            )
            outs.append(parts_ref[member, rows, :].astype(F32))
        top = functools.reduce(jnp.maximum, lses)
        shares = [jnp.exp2(lse - top) for lse in lses]
        weighted = sum(share * part for share, part in zip(shares, outs))
        merged = weighted / sum(shares)
        at = 0
        for far in range(4):
            for frame in range(frames):
                for row in range(tile_h):
                    first = (far * 4 + place) * tile_w
                    grid[frame, row, first : first + tile_w, :] = merged[at : at + tile_w]
                    at += tile_w
    out[...] = grid[...].astype(BF)


def combine(slots, info, parts, own, shape):
    smem = pl.BlockSpec(memory_space=pltpu.SMEM)
    return pl.pallas_call(
        combine_kernel,
        out_shape=jax.ShapeDtypeStruct(shape, BF),
        in_specs=[smem, smem, vmem(), hbm()],
        out_specs=vmem(),
        scratch_shapes=[
            pltpu.VMEM(shape, F32),
            pltpu.VMEM(own.shape, F32),
            pltpu.SemaphoreType.DMA,
        ],
        compiler_params=params(8),
        name="combine",
    )(slots, info, parts, keep(own))


def on_device(latents, prompt_rows, peg_weight, modulation_weight, qkv_weight, text_len, timestep):
    frames, tile_h, tile_w, width = latents.shape[1:]
    head_width = qkv_weight.shape[2]
    zl_at = lax.axis_index("zl")
    x_at = lax.axis_index("x")
    member = lax.axis_index("v") * 2 + zl_at

    row_axes = ("u", "v", "zl")
    padded = with_halo(latents, ((row_axes, 2),), 1)
    padded, peg_weight, modulation_weight = lax.optimization_barrier(
        (padded, peg_weight, modulation_weight)
    )
    padded = with_halo(padded, ((("zh", "x"), 3),), 1)
    shard = qkv_weight.reshape(qkv_weight.shape[0], 3 * head_width)
    weight = lax.all_gather(shard, ("item",) + row_axes, axis=0, tiled=True)
    summed = latents.astype(F32)
    for row_tap in range(3):
        for col_tap in range(3):
            summed = summed + padded[
                :, :, row_tap : row_tap + tile_h, col_tap : col_tap + tile_w, :
            ].astype(F32) * peg_weight[row_tap, col_tap].astype(F32)
    peg = summed.astype(BF).reshape(frames * tile_h * tile_w, width)

    activation = jax.nn.silu(time_angles(timestep[0], modulation_weight.shape[0])).astype(BF)
    own_columns = jnp.dot(activation[None, :], modulation_weight, preferred_element_type=F32)
    rest = own_columns.reshape(3, 128)
    terms = []
    for _ in range(3):
        terms.append(lax.reduce_precision(rest, 8, 7))
        rest = rest - terms[-1]
    extra = jnp.concatenate(terms).astype(BF)
    extra = jnp.pad(extra, ((0, peg.shape[0] - 9), (0, 0)))
    peg = jnp.concatenate([peg, extra], axis=1)

    tokens = lax.all_gather(peg, "zh", axis=0, tiled=True)
    half = tokens.shape[0] // 2
    low, high = tokens[:half], tokens[half:]
    up = [(i, (i + 1) % 4) for i in range(4)]
    down = [(i, (i - 1) % 4) for i in range(4)]
    a0, b1 = lax.ppermute(low, "x", up), lax.ppermute(high, "x", down)
    a1, b0 = lax.ppermute(high, "x", up), lax.ppermute(low, "x", down)
    a0, b1 = lax.optimization_barrier((a0, b1))
    c0, c1 = lax.ppermute(a0, "x", up), lax.ppermute(b1, "x", down)
    pieces = (low, high, a0, a1, b0, b1, c0, c1)
    distance = (jnp.arange(4, dtype=jnp.int32) - x_at) % 4
    slots = jnp.where(distance == 0, 0, jnp.where(distance == 3, 1, distance + 1))

    lower = member * TEXT_PART
    start = jnp.minimum(lower, prompt_rows.shape[1] - TEXT_PART)
    text_rows = lax.dynamic_slice_in_dim(prompt_rows[0], start, TEXT_PART, axis=0)
    queries, kv, text_kv = project(slots, pieces, text_rows, weight)
    group = ("v", "zl")
    swaps = (
        ("zl", [(0, 1), (1, 0)]),
        ("v", [(0, 1), (1, 0)]),
        (group, [(0, 3), (3, 0), (1, 2), (2, 1)]),
    )
    qs = [lax.ppermute(queries, axis, swap) for axis, swap in swaps]
    near = [lax.ppermute(kv, "u", up), lax.ppermute(kv, "u", down)]
    near = lax.optimization_barrier(near)
    count = kv.shape[0]
    far = [
        lax.ppermute(near[0][: count // 2], "u", up),
        lax.ppermute(near[1][count // 2 :], "u", down),
    ]
    info = jnp.stack([start, lower, text_len[0], member])
    shape = (3, 2, count, 128)
    first = jax.ShapeDtypeStruct(shape, F32)
    first = attend(first_kernel, "first", 3, first, None, info, qs, [kv, *near], text_kv)
    shape = (4, count + count // 128 * STAT_ROWS, 128)
    parts = jax.ShapeDtypeStruct(shape, BF)
    parts = attend(rest_kernel, "rest", 3, parts, (3,) + shape[1:], info, qs, far, None, first)
    parts = lax.all_to_all(parts, group, split_axis=0, concat_axis=0, tiled=True)
    shape = (2, count, 128)
    own = jax.ShapeDtypeStruct(shape, F32)
    own = attend(own_kernel, "own", 1, own, shape, info, [queries], [kv, *near, *far], text_kv)
    shape = (frames, tile_h, 16 * tile_w, head_width)
    return combine(slots, info, parts, own, shape)[None]


def solution(mesh):
    fine = Mesh(mesh.devices.reshape(2, 4, 2, 2, 4, 4), ("item", "u", "v", "zl", "zh", "x"))
    row = ("u", "v", "zl")
    col = ("zh", "x")
    in_specs = (
        P("item", None, row, col, None),
        P("item", None, None),
        P(),
        P(None, col),
        P(("item",) + row, None, col),
        P("item"),
        P("item"),
    )
    out_specs = P("item", None, row, None, col)
    return jax.shard_map(
        on_device, mesh=fine, in_specs=in_specs, out_specs=out_specs, check_vma=False
    )
```

```python
import functools
import math

import jax
import jax.numpy as jnp
from jax import lax
from jax.experimental import pallas as pl
from jax.experimental.pallas import tpu as pltpu
from jax.sharding import Mesh, PartitionSpec as P

HD = 64
LOG2E = 1.4426950408889634
SCALE2 = 0.125 * LOG2E
BF = jnp.bfloat16
F32 = jnp.float32
TEXT_PART = 64
STAT_ROWS = 16


def vmem(*shape):
    return pl.BlockSpec(memory_space=pltpu.VMEM)


def hbm():
    return pl.BlockSpec(memory_space=pltpu.MemorySpace.HBM)


def keep(x):
    return pltpu.with_memory_space_constraint(x, pltpu.MemorySpace.HBM)


def params(mib):
    return pltpu.CompilerParams(vmem_limit_bytes=mib << 20)


def with_halo(block, sides, width):
    for axis, dim in sides:
        count = lax.axis_size(axis)
        forward = [(i, i + 1) for i in range(count - 1)]
        backward = [(target, source) for source, target in forward]
        low = lax.ppermute(
            lax.slice_in_dim(block, block.shape[dim] - width, None, axis=dim), axis, forward
        )
        high = lax.ppermute(lax.slice_in_dim(block, 0, width, axis=dim), axis, backward)
        block = jnp.concatenate([low, block, high], axis=dim)
    return block


def time_angles(step, count):
    half = count // 2
    freqs = jnp.exp(-math.log(10000.0) * jnp.arange(half, dtype=F32) / half)
    angle = step.astype(F32) * freqs
    return jnp.concatenate([jnp.cos(angle), jnp.sin(angle)])


def project_kernel(
    slots, x0, x1, a0, a1, b0, b1, c0, c1, text, w_hbm,
    q_out, kv_out, text_out,
    held, mod, extra, normed, w_ref, in_sems, w_sem,
):
    half = x0.shape[0]
    rows = 2 * half
    width = text.shape[1]
    tile = rows // 4
    arrived = []
    for slot, (low, high) in enumerate(((x0, x1), (a0, a1), (b0, b1), (c0, c1))):
        arrived += [(low, slot * rows), (high, slot * rows + half)]

    def tail(i):
        piece, at = arrived[i]
        size = piece.shape[0]
        return pltpu.make_async_copy(
            piece.at[:, pl.ds(width, 128)], extra.at[pl.ds(at, size), :], in_sems.at[0, i]
        )

    def body(i):
        piece, at = arrived[i]
        size = piece.shape[0]
        return pltpu.make_async_copy(
            piece.at[:, pl.ds(0, width)], held.at[pl.ds(at, size), :], in_sems.at[1, i]
        )

    count = len(arrived)
    for i in range(count):
        tail(i).start()
    for i in range(count):
        body(i).start()
    fetch = pltpu.make_async_copy(w_hbm, w_ref, w_sem)
    fetch.start()
    for i in range(count):
        tail(i).wait()
    for place in range(4):
        base = pl.multiple_of(slots[place] * rows, rows)
        terms = extra[pl.ds(base, rows), :].astype(F32)
        for far in range(4):
            for chunk in range(3):
                at = (far * 4 + place) * 3 + chunk
                kind, first = divmod(at * 128, width)
                row = far * tile + chunk
                mod[kind : kind + 1, first : first + 128] = (
                    terms[row : row + 1] + terms[row + 3 : row + 4] + terms[row + 6 : row + 7]
                )
    shift = mod[0:1, :]
    gain = 1.0 + mod[1:2, :]

    def norm(rows_in, at):
        values = rows_in.astype(F32)
        center = jnp.sum(values, axis=1, keepdims=True) * (1.0 / width)
        centered = values - center
        spread = jnp.sum(centered * centered, axis=1, keepdims=True) * (1.0 / width)
        result = centered * lax.rsqrt(spread + 1e-06) * gain + shift
        normed[at : at + rows_in.shape[0], :] = result.astype(BF)

    norm(text[...], 4 * rows)
    for part in range(2):
        first = 2 * rows * part
        for i in range(count):
            if first <= arrived[i][1] < first + 2 * rows:
                body(i).wait()
        for block in (2 * part, 2 * part + 1):
            norm(held[block * rows : (block + 1) * rows, :], block * rows)
        last = first + 2 * rows + (text.shape[0] if part else 0)
        if part == 0:
            fetch.wait()
        out = jnp.dot(normed[first:last, :], w_ref[...], preferred_element_type=F32).astype(BF)
        span = pl.ds(first, 2 * rows)
        q_out[span, :] = out[: 2 * rows, :128]
        kv_out[span, :] = out[: 2 * rows, 128:]
        if part:
            text_out[...] = out[2 * rows :, 128:]


def project(slots, pieces, text, weight):
    half, lanes = pieces[0].shape
    rows = 2 * half
    width = text.shape[1]
    return pl.pallas_call(
        project_kernel,
        out_shape=[
            jax.ShapeDtypeStruct((4 * rows, 128), BF),
            jax.ShapeDtypeStruct((4 * rows, 256), BF),
            jax.ShapeDtypeStruct((text.shape[0], 256), BF),
        ],
        in_specs=[pl.BlockSpec(memory_space=pltpu.SMEM)] + [hbm()] * 8 + [vmem(), hbm()],
        out_specs=[vmem()] * 3,
        scratch_shapes=[
            pltpu.VMEM((4 * rows, width), BF),
            pltpu.VMEM((2, width), F32),
            pltpu.VMEM((4 * rows, 128), BF),
            pltpu.VMEM((4 * rows + text.shape[0], width), BF),
            pltpu.VMEM(weight.shape, BF),
            pltpu.SemaphoreType.DMA((2, 8)),
            pltpu.SemaphoreType.DMA,
        ],
        compiler_params=params(28),
        cost_estimate=pl.CostEstimate(
            flops=8 * rows * width * weight.shape[1],
            bytes_accessed=2 * (4 * rows * lanes + weight.size),
            transcendentals=4 * rows,
        ),
        name="project",
    )(slots, *map(keep, pieces), text, keep(weight))


def load_keys(blocks, text_kv, keys, values):
    at = 0
    for block in blocks:
        size = block.shape[0]
        keys[at : at + size, :] = block[:, :128]
        values[at : at + size, :128] = block[:, 128:]
        at += size
    if text_kv is not None:
        pad = 128 - TEXT_PART
        keys[at : at + TEXT_PART, :] = text_kv[:, :128]
        keys[at + TEXT_PART :, :] = jnp.zeros((pad, 128), BF)
        values[at : at + TEXT_PART, :128] = text_kv[:, 128:]
        values[at + TEXT_PART :, :128] = jnp.zeros((pad, 128), BF)
    values[:, 128:] = jnp.ones((values.shape[0], 128), BF)


def softmax_block(info, q, keys, values, has_text):
    rows = q.shape[0]
    latent = keys.shape[0] - (128 if has_text else 0)
    lane = lax.broadcasted_iota(jnp.int32, (rows, 128), 1)
    position = info[0] + lane
    valid = (position >= info[1]) & (position < info[2]) & (lane < TEXT_PART)
    q = q.astype(F32)
    accs, tops = [], []
    for head in range(2):
        own = jnp.where(lane // HD == head, q, 0.0).astype(BF)
        s = lax.dot_general(
            own, keys[...], (((1,), (1,)), ((), ())), preferred_element_type=F32
        )
        top = jnp.max(s[:, :latent], axis=1, keepdims=True)
        if has_text:
            text = jnp.where(valid, s[:, latent:], -1e30)
            top = jnp.maximum(top, jnp.max(text, axis=1, keepdims=True))
        top = top * SCALE2
        p = jnp.exp2(s[:, :latent] * SCALE2 - top).astype(BF)
        if has_text:
            p_text = jnp.where(valid, jnp.exp2(text * SCALE2 - top), 0.0).astype(BF)
            p = jnp.concatenate([p, p_text], axis=1)
        accs.append(jnp.dot(p, values[...], preferred_element_type=F32))
        tops.append(top)
    total = jnp.where(lane < HD, accs[0][:, 128:], accs[1][:, 128:])
    weighted = jnp.where(lane < HD, accs[0][:, :128], accs[1][:, :128])
    return weighted / total, jnp.where(lane < HD, tops[0], tops[1]) + jnp.log(total) * LOG2E


def first_kernel(info, q1, q2, q3, kv0, kv1, kv2, text_kv, o_ref, keys, values):
    load_keys((kv0, kv1, kv2), text_kv, keys, values)
    for i, q_ref in enumerate((q1, q2, q3)):
        o_ref[i, 0], o_ref[i, 1] = softmax_block(info, q_ref[...], keys, values, True)


def rest_kernel(
    info, q1, q2, q3, kv3, before, o_ref, keys, values, held, sems
):
    count = q1.shape[0]
    load_keys((kv3,), None, keys, values)
    term = lax.broadcasted_iota(jnp.int32, (STAT_ROWS, 128), 0)
    lane = lax.broadcasted_iota(jnp.int32, (STAT_ROWS, 128), 1)
    sends = []
    for i, q_ref in enumerate((q1, q2, q3)):
        member = jnp.bitwise_xor(info[3], i + 1)
        out, lse = softmax_block(info, q_ref[...], keys, values, False)
        earlier = before[i, 1]
        top = jnp.maximum(lse, earlier)
        new, old = jnp.exp2(lse - top), jnp.exp2(earlier - top)
        total = new + old
        held[i, :count, :] = ((new * out + old * before[i, 0]) / total).astype(BF)
        lse = top + jnp.log(total) * LOG2E
        across = jnp.zeros((STAT_ROWS, count), F32)
        for part in range(3):
            piece = lse.astype(BF)
            lse = lse - piece.astype(F32)
            pick = jnp.where((term % 8 == part) & (lane == term // 8 * HD), 1.0, 0.0).astype(BF)
            across = across + lax.dot_general(
                pick, piece, (((1,), (1,)), ((), ())), preferred_element_type=F32
            )
        for tile in range(count // 128):
            at = count + tile * STAT_ROWS
            held[i, at : at + STAT_ROWS, :] = across[:, tile * 128 : (tile + 1) * 128].astype(BF)
        sends.append(pltpu.make_async_copy(held.at[i], o_ref.at[member], sems.at[i]))
        sends[-1].start()
    for send in sends:
        send.wait()


def own_kernel(info, q_ref, kv0, kv1, kv2, kv3, text_kv, o_ref, keys, values, held, sems):
    load_keys((kv0, kv1, kv2, kv3), text_kv, keys, values)
    held[0], held[1] = softmax_block(info, q_ref[...], keys, values, True)
    copy = pltpu.make_async_copy(held, o_ref, sems.at[0])
    copy.start()
    copy.wait()


def attend(kernel, name, peers, out_shape, held, info, qs, blocks, text_kv=None, before=None):
    keys = sum(block.shape[0] for block in blocks) + (0 if text_kv is None else 128)
    count = qs[0].shape[0]
    operands = [*qs, *blocks] + [x for x in (text_kv, before) if x is not None]
    scratch = [pltpu.VMEM((keys, 128), BF), pltpu.VMEM((keys, 256), BF)]
    out_spec = vmem()
    if held is not None:
        scratch += [pltpu.VMEM(held, out_shape.dtype), pltpu.SemaphoreType.DMA((3,))]
        out_shape, out_spec = pltpu.MemorySpace.HBM(out_shape.shape, out_shape.dtype), hbm()
    return pl.pallas_call(
        kernel,
        out_shape=out_shape,
        in_specs=[pl.BlockSpec(memory_space=pltpu.SMEM)] + [vmem()] * len(operands),
        out_specs=out_spec,
        scratch_shapes=scratch,
        compiler_params=params(24),
        cost_estimate=pl.CostEstimate(
            flops=4 * peers * count * keys * 256,
            bytes_accessed=512 * (peers * count + keys),
            transcendentals=2 * peers * count * keys,
        ),
        name=name,
    )(info, *operands)


def combine_kernel(slots, info, parts_ref, own_hbm, out, grid, own, sem):
    copy = pltpu.make_async_copy(own_hbm, own, sem)
    copy.start()
    o_ref, l_ref = own.at[0], own.at[1]
    members = parts_ref.shape[0]
    block = 128
    count = o_ref.shape[0]
    term = lax.broadcasted_iota(jnp.int32, (STAT_ROWS, 128), 0)
    head = lax.broadcasted_iota(jnp.int32, (STAT_ROWS, 128), 1) // HD
    spread = jnp.where((term // 8 == head) & (term % 8 < 3), 1.0, 0.0).astype(BF)
    frames, tile_h, cells = out.shape[:3]
    tile_w = cells // 16
    copy.wait()
    for place in range(4):
        slot = slots[place]
        rows = pl.ds(pl.multiple_of(slot * block, block), block)
        at = pl.ds(pl.multiple_of(count + slot * STAT_ROWS, STAT_ROWS), STAT_ROWS)
        lses = [l_ref[rows, :]]
        outs = [o_ref[rows, :]]
        for step in range(1, members):
            member = jnp.bitwise_xor(info[3], step)
            lses.append(
                lax.dot_general(
                    parts_ref[member, at, :],
                    spread,
                    (((0,), (0,)), ((), ())),
                    preferred_element_type=F32,
                )
            )
            outs.append(parts_ref[member, rows, :].astype(F32))
        top = functools.reduce(jnp.maximum, lses)
        shares = [jnp.exp2(lse - top) for lse in lses]
        weighted = sum(share * part for share, part in zip(shares, outs))
        merged = weighted / sum(shares)
        at = 0
        for far in range(4):
            for frame in range(frames):
                for row in range(tile_h):
                    first = (far * 4 + place) * tile_w
                    grid[frame, row, first : first + tile_w, :] = merged[at : at + tile_w]
                    at += tile_w
    out[...] = grid[...].astype(BF)


def combine(slots, info, parts, own, shape):
    smem = pl.BlockSpec(memory_space=pltpu.SMEM)
    return pl.pallas_call(
        combine_kernel,
        out_shape=jax.ShapeDtypeStruct(shape, BF),
        in_specs=[smem, smem, vmem(), hbm()],
        out_specs=vmem(),
        scratch_shapes=[
            pltpu.VMEM(shape, F32),
            pltpu.VMEM(own.shape, F32),
            pltpu.SemaphoreType.DMA,
        ],
        compiler_params=params(8),
        name="combine",
    )(slots, info, parts, keep(own))


def on_device(latents, prompt_rows, peg_weight, modulation_weight, qkv_weight, text_len, timestep):
    frames, tile_h, tile_w, width = latents.shape[1:]
    head_width = qkv_weight.shape[2]
    zl_at = lax.axis_index("zl")
    x_at = lax.axis_index("x")
    member = lax.axis_index("v") * 2 + zl_at

    row_axes = ("u", "v", "zl")
    padded = with_halo(latents, ((row_axes, 2),), 1)
    padded, peg_weight, modulation_weight = lax.optimization_barrier(
        (padded, peg_weight, modulation_weight)
    )
    padded = with_halo(padded, ((("zh", "x"), 3),), 1)
    shard = qkv_weight.reshape(qkv_weight.shape[0], 3 * head_width)
    weight = lax.all_gather(shard, ("item",) + row_axes, axis=0, tiled=True)
    summed = latents.astype(F32)
    for row_tap in range(3):
        for col_tap in range(3):
            summed = summed + padded[
                :, :, row_tap : row_tap + tile_h, col_tap : col_tap + tile_w, :
            ].astype(F32) * peg_weight[row_tap, col_tap].astype(F32)
    peg = summed.astype(BF).reshape(frames * tile_h * tile_w, width)

    activation = jax.nn.silu(time_angles(timestep[0], modulation_weight.shape[0])).astype(BF)
    own_columns = jnp.dot(activation[None, :], modulation_weight, preferred_element_type=F32)
    rest = own_columns.reshape(3, 128)
    terms = []
    for _ in range(3):
        terms.append(lax.reduce_precision(rest, 8, 7))
        rest = rest - terms[-1]
    extra = jnp.concatenate(terms).astype(BF)
    extra = jnp.pad(extra, ((0, peg.shape[0] - 9), (0, 0)))
    peg = jnp.concatenate([peg, extra], axis=1)

    tokens = lax.all_gather(peg, "zh", axis=0, tiled=True)
    half = tokens.shape[0] // 2
    low, high = tokens[:half], tokens[half:]
    up = [(i, (i + 1) % 4) for i in range(4)]
    down = [(i, (i - 1) % 4) for i in range(4)]
    a0, b1 = lax.ppermute(low, "x", up), lax.ppermute(high, "x", down)
    a1, b0 = lax.ppermute(high, "x", up), lax.ppermute(low, "x", down)
    a0, b1 = lax.optimization_barrier((a0, b1))
    c0, c1 = lax.ppermute(a0, "x", up), lax.ppermute(b1, "x", down)
    pieces = (low, high, a0, a1, b0, b1, c0, c1)
    distance = (jnp.arange(4, dtype=jnp.int32) - x_at) % 4
    slots = jnp.where(distance == 0, 0, jnp.where(distance == 3, 1, distance + 1))

    lower = member * TEXT_PART
    start = jnp.minimum(lower, prompt_rows.shape[1] - TEXT_PART)
    text_rows = lax.dynamic_slice_in_dim(prompt_rows[0], start, TEXT_PART, axis=0)
    queries, kv, text_kv = project(slots, pieces, text_rows, weight)
    group = ("v", "zl")
    swaps = (
        ("zl", [(0, 1), (1, 0)]),
        ("v", [(0, 1), (1, 0)]),
        (group, [(0, 3), (3, 0), (1, 2), (2, 1)]),
    )
    qs = [lax.ppermute(queries, axis, swap) for axis, swap in swaps]
    near = [lax.ppermute(kv, "u", up), lax.ppermute(kv, "u", down)]
    far = lax.ppermute(kv, "u", [(i, (i + 2) % 4) for i in range(4)])
    count = kv.shape[0]
    info = jnp.stack([start, lower, text_len[0], member])
    shape = (3, 2, count, 128)
    first = jax.ShapeDtypeStruct(shape, F32)
    first = attend(first_kernel, "first", 3, first, None, info, qs, [kv, *near], text_kv)
    shape = (4, count + count // 128 * STAT_ROWS, 128)
    parts = jax.ShapeDtypeStruct(shape, BF)
    parts = attend(rest_kernel, "rest", 3, parts, (3,) + shape[1:], info, qs, [far], None, first)
    parts = lax.all_to_all(parts, group, split_axis=0, concat_axis=0, tiled=True)
    shape = (2, count, 128)
    own = jax.ShapeDtypeStruct(shape, F32)
    own = attend(own_kernel, "own", 1, own, shape, info, [queries], [kv, *near, far], text_kv)
    shape = (frames, tile_h, 16 * tile_w, head_width)
    return combine(slots, info, parts, own, shape)[None]


def solution(mesh):
    fine = Mesh(mesh.devices.reshape(2, 4, 2, 2, 4, 4), ("item", "u", "v", "zl", "zh", "x"))
    row = ("u", "v", "zl")
    col = ("zh", "x")
    in_specs = (
        P("item", None, row, col, None),
        P("item", None, None),
        P(),
        P(None, col),
        P(("item",) + row, None, col),
        P("item"),
        P("item"),
    )
    out_specs = P("item", None, row, None, col)
    return jax.shard_map(
        on_device, mesh=fine, in_specs=in_specs, out_specs=out_specs, check_vma=False
    )
```
